32 devices in a mesh: grp: 2 (over y), dev: 16 (over z, x, core).
Axes of the slice: x: 2, y: 2, z: 4, core: 2. Of those that a mesh axis runs over, the one named last changes fastest.
Arguments:
- series: float32 [2, 1024, 32768], P(None, None, ('grp', 'dev')), may hold values from -6 to 6
- templates: float32 [200, 128], replicated, may hold values from -0.5 to 0.5
- drift_template: int32 [16], replicated, may hold values from 0 to 199
- drift_reach: int32 [16], replicated, may hold values from 4 to 32, as said below
Outputs:
- powers: float32 [16, 33554432], P(None, ('grp', 'dev'))
The draws below stay inside these ranges and needn't reach their ends.
Inputs may be any that keep to these rules, and one draw needn't show every extreme that they name: Drift d uses the taps t with 32 - drift_reach[d] <= t < 32 + drift_reach[d]; some drift uses all 64 taps.
All inputs are finite; a program needn't handle non-finite values.
Results may differ from the reference program's by a relative error of at most 0.000078.
Values sent between devices are 32-bit elements; how exact they have to be, the bound alone decides.
No kernel may reach another device: no remote copies, remote signals or barrier semaphores. Data moves between devices by JAX's collectives and lax.ppermute only.
A program may use at most 320 MiB of HBM per device.

```python
import math
import jax
import jax.numpy as jnp
from jax import lax

P1 = 32
P2 = 32
Q1 = 128
Q2 = 256
P_SIZE = 1024
Q = 32768
TAPS = 64
TEMPLATES = 200
DRIFTS = 16


def draw_drift_reach(key, part):
    draw_key, spot_key = jax.random.split(jax.random.fold_in(key, 11))
    values = jax.random.randint(draw_key, (DRIFTS,), 4, TAPS // 2 + 1)
    chosen = jax.random.randint(spot_key, (), 0, DRIFTS)
    return jnp.where(jnp.arange(DRIFTS) == chosen, TAPS // 2, values).astype(jnp.int32)


def with_ends(entries, own_key, smallest, largest):
    shape = entries.shape
    spot = [jax.random.randint(jax.random.fold_in(own_key, axis), (), 0, shape[axis]) for axis in range(len(shape))]
    entries = entries.at[tuple(spot)].set(smallest)
    longest = shape.index(max(shape))
    spot[longest] = (spot[longest] + 1) % shape[longest]
    return entries.at[tuple(spot)].set(largest)


def levels(rng, shape, pieces, smallest, top_value):
    def one(position, blocks):
        draws = jax.random.uniform(jax.random.fold_in(jax.random.fold_in(rng, 6), position), (blocks,), jnp.float32, smallest / len(pieces), top_value / len(pieces))
        return jnp.repeat(jnp.exp(draws), shape[position] // blocks).reshape((-1,) + (1,) * (len(shape) - position - 1))

    factor_of = one(*pieces[0])
    for cut in pieces[1:]:
        factor_of = factor_of * one(*cut)
    return factor_of


def gaussian(stream_key, dims, width, reach, cuts=(), kind=jnp.bfloat16):
    drawn = jax.random.normal(stream_key, dims, jnp.float32) * width
    if len(cuts) > 0:
        drawn = levels(stream_key, dims, cuts, -0.22, 0.18) * drawn
    return jnp.clip(drawn, min=-reach, max=reach).astype(kind)


def setup_inputs(seed: int = 0) -> dict:
    keys = jax.random.split(jax.random.key(seed), 5)
    series = gaussian(keys[0], (2, P_SIZE, Q), 1.0, 6.0, ((2, 32),), jnp.float32)
    templates = gaussian(keys[1], (TEMPLATES, 2 * TAPS), (2 * TAPS) ** -0.5, 0.5, (), jnp.float32)
    drift_template = with_ends(jax.random.randint(keys[2], (DRIFTS,), 0, TEMPLATES), jax.random.fold_in(keys[2], 1), 0, TEMPLATES - 1).astype(jnp.int32)
    drift_reach = draw_drift_reach(jax.random.fold_in(keys[4], 71), 0)
    return {"series": series, "templates": templates, "drift_template": drift_template, "drift_reach": drift_reach}


def tap_kernels(templates, drift_template, drift_reach):
    chosen = templates[drift_template]
    taps_index = jnp.arange(TAPS, dtype=jnp.int32)[None, :]
    center = TAPS // 2
    inside = ((taps_index >= center - drift_reach[:, None]) & (taps_index < center + drift_reach[:, None])).astype(templates.dtype)
    return (chosen[:, :TAPS] * inside, chosen[:, TAPS:] * inside)

def banded(kernel_rows, window_width):
    lane_width = 128
    drift_count = kernel_rows.shape[0]
    padded = jnp.concatenate([kernel_rows, jnp.zeros((drift_count, window_width + 1 - TAPS), kernel_rows.dtype)], axis=1)
    tiled_rows = jnp.tile(padded, (1, lane_width))[:, :lane_width * window_width]
    return jnp.swapaxes(tiled_rows.reshape(drift_count, lane_width, window_width), 1, 2)

def reference(series, templates, drift_template, drift_reach):
    sample_count = 2 * P1 * P2 * Q1 * Q2
    samples = jnp.transpose(series, (1, 2, 0)).reshape(sample_count)
    bin_count = sample_count // 2
    spectrum = jnp.fft.rfft(samples)[:bin_count] / math.sqrt(sample_count)
    half_taps = TAPS // 2
    lane_width = 128
    window_width = lane_width + TAPS
    row_count = bin_count // lane_width
    extended = jnp.stack([jnp.pad(jnp.real(spectrum), (half_taps, half_taps)), jnp.pad(jnp.imag(spectrum), (half_taps, half_taps))])
    head_rows = extended[:, :bin_count].reshape(2, row_count, lane_width)
    rest_bins = jnp.concatenate([extended[:, lane_width:], jnp.zeros((2, lane_width - TAPS), extended.dtype)], axis=1)
    tail_rows = rest_bins.reshape(2, row_count, lane_width)[:, :, :TAPS]
    windows = jnp.concatenate([head_rows, tail_rows], axis=2)
    flat_windows = jnp.concatenate([windows[0], windows[1]], axis=1)
    kernel_real, kernel_imag = tap_kernels(templates, drift_template, drift_reach)
    band_real = banded(kernel_real, window_width)
    band_imag = banded(kernel_imag, window_width)
    matrices = jnp.concatenate([jnp.concatenate([band_real, band_imag], axis=2), jnp.concatenate([-band_imag, band_real], axis=2)], axis=1)

    def one_drift(matrix):
        response = jnp.dot(flat_windows, matrix, precision=lax.Precision.HIGHEST, preferred_element_type=jnp.float32)
        power_rows = response[:, :lane_width] * response[:, :lane_width] + response[:, lane_width:] * response[:, lane_width:]
        return power_rows.reshape(row_count * lane_width)
    return lax.map(one_drift, matrices)
```

```python
import functools
import math

import jax
import jax.numpy as jnp
from jax import lax
from jax.experimental import pallas as pl
from jax.experimental.pallas import tpu as pltpu
from jax.sharding import PartitionSpec as P

AXES = ("grp", "dev")
LANES = 128
SUBLANES = 8
VMEM_LIMIT = 60 * 1024 * 1024
F32 = jnp.float32
BF16 = jnp.bfloat16


def split(x):
    high = x.astype(BF16)
    return high, (x - high.astype(F32)).astype(BF16)


def split_xla(x):
    high = lax.reduce_precision(x, 8, 7)
    return high.astype(BF16), lax.reduce_precision(x - high, 8, 7).astype(BF16)


def phases(product, length):
    angles = (product % length).astype(F32) * (2.0 * math.pi / length)
    return jnp.cos(angles), jnp.sin(angles)


def iota(count):
    return jnp.arange(count, dtype=jnp.int32)


P1 = 32
P2 = 32
Q1 = 128
Q2 = 256
N = 67108864
M = 33554432
TAPS = 64
HIGHEST = lax.Precision.HIGHEST


def extended_2(block, sides, width):
    for axis, dim in sides:
        count = lax.axis_size(axis)
        forward = [(i, i + 1) for i in range(count - 1)]
        backward = [(target, source) for source, target in forward]
        low = lax.ppermute(
            lax.slice_in_dim(block, block.shape[dim] - width, None, axis=dim), axis, forward
        )
        high = lax.ppermute(lax.slice_in_dim(block, 0, width, axis=dim), axis, backward)
        block = jnp.concatenate([low, block, high], axis=dim)
    return block


def dft_table(length):
    indices = jnp.arange(length, dtype=jnp.int32)
    product = indices[:, None] * indices[None, :] % length
    angles = product.astype(jnp.float32) * (-2.0 * math.pi / length)
    return (jnp.cos(angles), jnp.sin(angles))


def twiddle(row_index, col_index, length):
    product = row_index[:, None] * col_index[None, :] % length
    angles = product.astype(jnp.float32) * (-2.0 * math.pi / length)
    return (jnp.cos(angles), jnp.sin(angles))


def complex_einsum(formula, left_pair, right_pair):
    left_real, left_imag = left_pair
    right_real, right_imag = right_pair
    real_part = jnp.einsum(formula, left_real, right_real, precision=HIGHEST) - jnp.einsum(
        formula, left_imag, right_imag, precision=HIGHEST
    )
    imag_part = jnp.einsum(formula, left_real, right_imag, precision=HIGHEST) + jnp.einsum(
        formula, left_imag, right_real, precision=HIGHEST
    )
    return (real_part, imag_part)


def complex_scale(values, factor):
    values_real, values_imag = values
    factor_real, factor_imag = factor
    return (
        values_real * factor_real - values_imag * factor_imag,
        values_real * factor_imag + values_imag * factor_real,
    )


def column_transform(series):
    col_count = series.shape[2]
    blocks = series.reshape(2, P1, P2, col_count)
    first_table = dft_table(P1)
    sectioned = (
        jnp.einsum("ja,eabc->ejbc", first_table[0], blocks, precision=HIGHEST),
        jnp.einsum("ja,eabc->ejbc", first_table[1], blocks, precision=HIGHEST),
    )
    inner_turn = twiddle(jnp.arange(P1, dtype=jnp.int32), jnp.arange(P2, dtype=jnp.int32), P1 * P2)
    sectioned = complex_scale(
        sectioned, (inner_turn[0][None, :, :, None], inner_turn[1][None, :, :, None])
    )
    sectioned = complex_einsum("kb,ejbc->ekjc", dft_table(P2), sectioned)
    return (
        sectioned[0].reshape(2, P1 * P2, col_count),
        sectioned[1].reshape(2, P1 * P2, col_count),
    )


def row_transform(values):
    parts_count, row_count = (values[0].shape[0], values[0].shape[1])
    shaped = (
        values[0].reshape(parts_count, row_count, Q1, Q2),
        values[1].reshape(parts_count, row_count, Q1, Q2),
    )
    sectioned = complex_einsum("ja,kbac->kbjc", dft_table(Q1), shaped)
    inner_turn = twiddle(jnp.arange(Q1, dtype=jnp.int32), jnp.arange(Q2, dtype=jnp.int32), Q1 * Q2)
    sectioned = complex_scale(sectioned, (inner_turn[0][None, None], inner_turn[1][None, None]))
    sectioned = complex_einsum("lc,kbjc->kblj", dft_table(Q2), sectioned)
    return (
        sectioned[0].reshape(parts_count, row_count, Q1 * Q2),
        sectioned[1].reshape(parts_count, row_count, Q1 * Q2),
    )


def combine_halves(even_part, odd_part, frequency):
    angles = frequency.astype(jnp.float32) * (-2.0 * math.pi / N)
    turned = complex_scale(odd_part, (jnp.cos(angles), jnp.sin(angles)))
    norm_scale = 1.0 / math.sqrt(N)
    return ((even_part[0] + turned[0]) * norm_scale, (even_part[1] + turned[1]) * norm_scale)


def to_rows(stacked):
    group_count = lax.axis_size("grp")
    member_count = lax.axis_size("dev")
    leading = stacked.shape[0]
    col_count = stacked.shape[2]
    row_count = stacked.shape[1] // (group_count * member_count)
    shaped = stacked.reshape(leading, group_count, member_count, row_count, 1, 1, col_count)
    arrived = lax.all_to_all(
        lax.all_to_all(shaped, "grp", split_axis=1, concat_axis=4, tiled=True),
        "dev",
        split_axis=2,
        concat_axis=5,
        tiled=True,
    )
    return arrived.reshape(leading, row_count, group_count * member_count * col_count)


def to_segments(stacked):
    group_count = lax.axis_size("grp")
    member_count = lax.axis_size("dev")
    leading = stacked.shape[0]
    row_count = stacked.shape[1]
    col_count = stacked.shape[2] // (group_count * member_count)
    shaped = stacked.reshape(leading, 1, 1, row_count, group_count, member_count, col_count)
    arrived = lax.all_to_all(
        lax.all_to_all(shaped, "grp", split_axis=4, concat_axis=1, tiled=True),
        "dev",
        split_axis=5,
        concat_axis=2,
        tiled=True,
    )
    gathered = arrived.reshape(leading, group_count * member_count * row_count, col_count)
    return jnp.swapaxes(gathered, 1, 2).reshape(
        leading, col_count * group_count * member_count * row_count
    )


def general_taps(templates, drift_template, drift_reach):
    template_count = templates.shape[0]
    selector = (
        drift_template[:, None] == jnp.arange(template_count, dtype=jnp.int32)[None, :]
    ).astype(jnp.float32)
    chosen = jnp.dot(selector, templates, precision=HIGHEST, preferred_element_type=jnp.float32)
    taps_index = jnp.arange(TAPS, dtype=jnp.int32)[None, :]
    center = TAPS // 2
    inside = (
        (taps_index >= center - drift_reach[:, None]) & (taps_index < center + drift_reach[:, None])
    ).astype(jnp.float32)
    return (chosen[:, :TAPS] * inside, chosen[:, TAPS:] * inside)


def general_banded(kernel_rows, window_width):
    lane_width = 128
    drift_count = kernel_rows.shape[0]
    padded = jnp.concatenate(
        [kernel_rows, jnp.zeros((drift_count, window_width + 1 - TAPS), jnp.float32)], axis=1
    )
    tiled_rows = jnp.tile(padded, (1, lane_width))[:, : lane_width * window_width]
    return jnp.swapaxes(tiled_rows.reshape(drift_count, lane_width, window_width), 1, 2)


def correlate(extended, kernels, segment_bins):
    lane_width = 128
    row_count = segment_bins // lane_width
    window_width = lane_width + TAPS
    head_rows = extended[:, :segment_bins].reshape(2, row_count, lane_width)
    rest_bins = jnp.concatenate(
        [extended[:, lane_width:], jnp.zeros((2, lane_width - TAPS), jnp.float32)], axis=1
    )
    tail_rows = rest_bins.reshape(2, row_count, lane_width)[:, :, :TAPS]
    windows = jnp.concatenate([head_rows, tail_rows], axis=2)
    flat_windows = jnp.concatenate([windows[0], windows[1]], axis=1)
    band_real = general_banded(kernels[0], window_width)
    band_imag = general_banded(kernels[1], window_width)
    matrices = jnp.concatenate(
        [
            jnp.concatenate([band_real, band_imag], axis=2),
            jnp.concatenate([-band_imag, band_real], axis=2),
        ],
        axis=1,
    )
    response = jnp.einsum(
        "rw,dwo->dro", flat_windows, matrices, precision=HIGHEST, preferred_element_type=jnp.float32
    )
    power_rows = (
        response[:, :, :lane_width] * response[:, :, :lane_width]
        + response[:, :, lane_width:] * response[:, :, lane_width:]
    )
    return power_rows.reshape(power_rows.shape[0], row_count * lane_width)


def general_local(series, templates, drift_template, drift_reach):
    position = lax.axis_index(("grp", "dev"))
    col_count = series.shape[2]
    row_total = P1 * P2
    row_frequency = jnp.arange(row_total, dtype=jnp.int32)
    columns = position * col_count + jnp.arange(col_count, dtype=jnp.int32)
    column_turn = twiddle(row_frequency, columns, M)
    section_real, section_imag = column_transform(series)
    turned = complex_scale(
        (section_real, section_imag), (column_turn[0][None], column_turn[1][None])
    )
    by_rows = to_rows(jnp.concatenate([turned[0], turned[1]], axis=0))
    spectrum = row_transform((by_rows[0:2], by_rows[2:4]))
    row_count = by_rows.shape[1]
    row_index = position * row_count + jnp.arange(row_count, dtype=jnp.int32)
    frequency = row_index[:, None] + row_total * jnp.arange(Q1 * Q2, dtype=jnp.int32)[None, :]
    whole_real, whole_imag = combine_halves(
        (spectrum[0][0], spectrum[1][0]), (spectrum[0][1], spectrum[1][1]), frequency
    )
    segment = to_segments(jnp.stack([whole_real, whole_imag]))
    segment_bins = segment.shape[1]
    kernels = general_taps(templates, drift_template, drift_reach)
    extended = extended_2(segment, ((("grp", "dev"), 1),), TAPS // 2)
    return correlate(extended, kernels, segment_bins)


def column_kernel(x_ref, table_ref, base_re_ref, base_im_ref, step_re_ref, step_im_ref, o_ref):
    slots = base_re_ref.shape[0]
    rows = x_ref.shape[1]
    width = x_ref.shape[2]
    block = pl.program_id(0)
    blocks = pl.num_programs(0)
    x = jnp.concatenate([x_ref[0], x_ref[1]], axis=1)
    high, low = split(x)
    out = jnp.dot(
        table_ref[...], jnp.concatenate([high, high], axis=0), preferred_element_type=F32
    ) + jnp.dot(table_ref[:, :rows], low, preferred_element_type=F32)
    base_re = base_re_ref[...]
    base_im = base_im_ref[...]
    for chunk in range(2 * width // LANES):
        lanes = slice(chunk * LANES, (chunk + 1) * LANES)
        step_re = step_re_ref[0, :, chunk : chunk + 1]
        step_im = step_im_ref[0, :, chunk : chunk + 1]
        turn_re = base_re * step_re - base_im * step_im
        turn_im = base_re * step_im + base_im * step_re
        real = out[:slots, lanes]
        imag = out[slots:, lanes]
        pitch = 2 * width // LANES * SUBLANES
        start = chunk * SUBLANES + block
        o_ref[pl.ds(start, slots, stride=pitch), :] = real * turn_re + imag * turn_im
        o_ref[pl.ds(start + blocks, slots, stride=pitch), :] = imag * turn_re - real * turn_im


def column_stage(series, position, width):
    rows, cols = series.shape[1], series.shape[2]
    slots = rows // 2
    blocks = cols // width
    samples = 2 * rows * cols * lax.axis_size(AXES)
    slot = iota(slots)
    near_re, near_im = phases(slot[:, None] * iota(LANES)[None, :], rows)
    far_re, far_im = phases(slot[:, None] * (LANES * iota(rows // LANES))[None, :], rows)
    cos = jnp.concatenate(
        [near_re * far_re[:, i : i + 1] - near_im * far_im[:, i : i + 1] for i in range(rows // LANES)],
        axis=1,
    )
    sin = jnp.concatenate(
        [near_re * far_im[:, i : i + 1] + near_im * far_re[:, i : i + 1] for i in range(rows // LANES)],
        axis=1,
    )
    alternating = (1 - 2 * (iota(rows) % 2)).astype(F32)[None, :]
    sin = jnp.where(slot[:, None] == 0, alternating, -sin)
    table = jnp.concatenate(split_xla(jnp.concatenate([cos, sin], axis=0)), axis=1)
    base_re, base_im = phases(slot[:, None] * (2 * iota(LANES))[None, :], samples)
    chunks = width // LANES
    start = (
        2 * (position * cols + width * iota(blocks)[:, None, None] + LANES * iota(chunks)[None, None, :])
        + iota(2)[None, :, None]
    ).reshape(blocks, 1, 2 * chunks)
    step_re, step_im = phases(start * slot[None, :, None], samples)
    small = pl.BlockSpec((1, slots, 2 * chunks), lambda i: (i, 0, 0))
    whole = lambda a: pl.BlockSpec(a.shape, lambda i: (0, 0))
    return pl.pallas_call(
        column_kernel,
        grid=(blocks,),
        in_specs=[
            pl.BlockSpec((2, rows, width), lambda i: (0, 0, i)),
            whole(table),
            whole(base_re),
            whole(base_im),
            small,
            small,
        ],
        out_specs=pl.BlockSpec((slots * 2 * chunks * SUBLANES, LANES), lambda i: (0, 0)),
        out_shape=jax.ShapeDtypeStruct((slots * 2 * chunks * SUBLANES, LANES), F32),
        compiler_params=pltpu.CompilerParams(vmem_limit_bytes=VMEM_LIMIT),
        name="columns",
    )(series, table, base_re, base_im, step_re, step_im)


def row_kernel(variant_ref, x_ref, first_ref, turn_ref, second_ref, o_ref):
    depth = first_ref.shape[2] // 3
    count, width = turn_ref.shape[3], turn_ref.shape[4]
    x = [x_ref[:, 0, i].reshape(depth, LANES) for i in range(width // LANES)]
    high, low = split(jnp.concatenate(x, axis=1))
    out = jnp.dot(
        first_ref[0], jnp.concatenate([high, high, low], axis=0), preferred_element_type=F32
    )
    pieces = []
    for side in range(2):
        real = out[2 * side * count : (2 * side + 1) * count]
        imag = out[(2 * side + 1) * count : (2 * side + 2) * count]
        turn_re = turn_ref[0, side, 0]
        turn_im = turn_ref[0, side, 1]
        turned = jnp.concatenate(
            [real * turn_re + imag * turn_im, imag * turn_re - real * turn_im], axis=1
        )
        high, low = split(turned)
        pieces.append(jnp.concatenate([high, high, low], axis=1))
    result = lax.dot_general(
        second_ref[...],
        jnp.concatenate(pieces, axis=0),
        (((1,), (1,)), ((), ())),
        preferred_element_type=F32,
    )
    half = result.shape[0] // 2
    for side in range(2):
        for part in range(2):
            block = result[part * half : (part + 1) * half, side * count : (side + 1) * count]
            o_ref[:, side, part, 0] = block.reshape(half // SUBLANES, SUBLANES, count)


def row_stage(arrived, position, total_rows, samples):
    devices, slots, chunks, sublanes, _ = arrived.shape
    width = chunks * LANES
    inner = sublanes // 2
    count = devices * inner
    lines = width // 2
    freq = iota(count)[:, None]
    order = (inner * iota(devices)[:, None] + iota(inner)[None, :]).reshape(1, devices, inner)
    fc, fs = phases(freq[:, :, None] * order, count)
    bc, bs = phases((freq[:, :, None] + 1) * order, count)
    hc, hs = phases((2 * freq[:, :, None] + 1) * order, 2 * count)
    zero = jnp.zeros_like(fc)
    pack = lambda on_re, on_im: jnp.stack([on_re, on_im], axis=2).reshape(count, devices * sublanes)
    usual = jnp.concatenate([pack(fc, fs), pack(-fs, fc), pack(bc, -bs), pack(-bs, -bc)], axis=0)
    special = jnp.concatenate(
        [pack(fc, zero), pack(-fs, zero), pack(zero, hc), pack(zero, -hs)], axis=0
    )
    high, low = split_xla(jnp.stack([usual, special]))
    first = jnp.concatenate([high, low, high], axis=2)
    beta = (2 * iota(lines)[None, :] + iota(2)[:, None]).reshape(1, width)
    length = count * width
    turn_a = jnp.stack(phases(freq * beta, length))
    turn_b = jnp.stack(phases((freq + 1) * beta, length))
    turn_c = jnp.stack(phases((2 * freq + 1) * beta, 2 * length))
    turn = jnp.stack([jnp.stack([turn_a, turn_b]), jnp.stack([turn_a, turn_c])])
    gc, gs = phases(iota(lines)[:, None] * beta, width)
    second = jnp.concatenate(
        [jnp.concatenate([gc, gs], axis=1), jnp.concatenate([-gs, gc], axis=1)], axis=0
    ) * (1.0 / math.sqrt(samples))
    high, low = split_xla(second)
    second = jnp.concatenate([high, low, high], axis=1)
    variant = jnp.where((iota(slots) == 0) & (position == 0), 1, 0).astype(jnp.int32)
    blocks = lines // SUBLANES
    shape = (blocks, 2, 2, slots, SUBLANES, count)
    return pl.pallas_call(
        row_kernel,
        grid_spec=pltpu.PrefetchScalarGridSpec(
            num_scalar_prefetch=1,
            grid=(slots,),
            in_specs=[
                pl.BlockSpec((devices, 1, chunks, sublanes, LANES), lambda i, v: (0, i, 0, 0, 0)),
                pl.BlockSpec((1,) + first.shape[1:], lambda i, v: (v[i], 0, 0)),
                pl.BlockSpec((1,) + turn.shape[1:], lambda i, v: (v[i], 0, 0, 0, 0)),
                pl.BlockSpec(second.shape, lambda i, v: (0, 0)),
            ],
            out_specs=pl.BlockSpec(
                (blocks, 2, 2, 1, SUBLANES, count), lambda i, v: (0, 0, 0, i, 0, 0)
            ),
        ),
        out_shape=jax.ShapeDtypeStruct(shape, F32),
        compiler_params=pltpu.CompilerParams(vmem_limit_bytes=VMEM_LIMIT),
        name="rows",
    )(variant, arrived, first, turn, second)


def band_kernel(taps_ref, o_ref):
    half = LANES // 2
    banded = []
    for drift in range(2):
        for part in range(2):
            line = jnp.broadcast_to(taps_ref[0, 2 * drift + part : 2 * drift + part + 1, :], (half, LANES))
            banded.append(pltpu.roll(line, 0, 1, stride=1, stride_axis=0))
    re = jnp.concatenate([banded[0], banded[2]], axis=0)
    im = jnp.concatenate([banded[1], banded[3]], axis=0)
    lines = jnp.concatenate(
        [jnp.concatenate([re, -im], axis=1), jnp.concatenate([im, re], axis=1)], axis=0
    )
    high, low = split(jnp.transpose(lines))
    o_ref[0] = jnp.concatenate([high, low, high], axis=0)


def band_stage(kernel_re, kernel_im):
    drifts, taps = kernel_re.shape
    lines = jnp.stack([kernel_re, kernel_im], axis=1)
    lines = jnp.pad(lines, ((0, 0), (0, 0), (0, LANES - taps))).reshape(drifts // 2, 4, LANES)
    return pl.pallas_call(
        band_kernel,
        grid=(drifts // 2,),
        in_specs=[pl.BlockSpec((1, 4, LANES), lambda i: (i, 0, 0))],
        out_specs=pl.BlockSpec((1, 6 * LANES, 2 * LANES), lambda i: (i, 0, 0)),
        out_shape=jax.ShapeDtypeStruct((drifts // 2, 6 * LANES, 2 * LANES), BF16),
        name="bands",
    )(lines)


def correlate_kernel(devices, slots, pad, x_ref, halo_ref, band_ref, o_ref, table, last, lhs):
    step = pl.program_id(0)
    steps = pl.num_programs(0)
    total = 2 * devices * slots
    pitch = total + pad
    half = LANES // 2
    taps_half = half // 2

    @pl.when(step == 0)
    def _():
        def source(s, carry):
            for side in range(2):
                for part in range(2):
                    for slot in range(slots):
                        tile = x_ref[
                            pl.ds(
                                pl.multiple_of(
                                    (((s * 2 + side) * 2 + part) * slots + slot) * SUBLANES, SUBLANES
                                ),
                                SUBLANES,
                            ),
                            :,
                        ]
                        row = s * slots + slot
                        if side == 1:
                            row = total - row
                            if slot == 0:
                                row = jnp.where(s == 0, total // 2, row)
                        table[pl.ds(part * SUBLANES * pitch + row, SUBLANES, stride=pitch), :] = tile
            return carry

        lax.fori_loop(0, devices, source, 0)
        last[...] = halo_ref[0:2, :]

    lane = lax.broadcasted_iota(jnp.int32, (LANES, LANES), 1)
    row_id = lax.broadcasted_iota(jnp.int32, (LANES, LANES), 0)
    blocks = total // LANES

    def turned(part, line, block):
        start = pl.multiple_of((part * SUBLANES + line) * pitch + block * LANES, SUBLANES)
        flat = jnp.transpose(table[pl.ds(start, LANES), :])
        return pltpu.roll(flat, taps_half, 1)

    next_line = jnp.minimum(step + 1, steps - 1)
    for part in range(2):
        rolled = [turned(part, step, block) for block in range(blocks)]
        follow = turned(part, next_line, 0)[0:1, :]
        follow = jnp.where(step == steps - 1, halo_ref[2 + part : 3 + part, :], follow)
        before = jnp.where(row_id == 0, last[part : part + 1, :], pltpu.roll(rolled[-1], 1, 0))
        after = jnp.where(row_id == LANES - 1, follow, pltpu.roll(rolled[0], LANES - 1, 0))
        last[part : part + 1, :] = rolled[-1][LANES - 1 : LANES, :]
        ext = []
        for block in range(blocks + 1):
            left = before if block == 0 else rolled[block - 1]
            right = after if block == blocks else rolled[block]
            ext.append(jnp.where(lane < taps_half, left, right))
        for block in range(blocks):
            odd = jnp.where(
                lane < half, pltpu.roll(ext[block], half, 1), pltpu.roll(ext[block + 1], half, 1)
            )
            for parity, window in enumerate((ext[block], odd)):
                high, low = split(window)
                rows = pl.ds((2 * block + parity) * LANES, LANES)
                lhs[rows, part * LANES : (part + 1) * LANES] = high
                lhs[rows, (2 + part) * LANES : (3 + part) * LANES] = high
                lhs[rows, (4 + part) * LANES : (5 + part) * LANES] = low

    pairs = band_ref.shape[0]
    group = 2
    chunks = blocks // group

    def multiply(index, carry):
        pair = index // chunks
        chunk = index % chunks
        rows = pl.ds(pl.multiple_of(chunk * group * 2 * LANES, LANES), group * 2 * LANES)
        out = jnp.dot(lhs[rows, :], band_ref[pair], preferred_element_type=F32)
        power = out[:, :LANES] * out[:, :LANES] + out[:, LANES:] * out[:, LANES:]
        outer = (2 * pair) // SUBLANES
        inner = (2 * pair) % SUBLANES
        for member in range(group):
            even = power[member * 2 * LANES : (member * 2 + 1) * LANES]
            odd = power[(member * 2 + 1) * LANES : (member * 2 + 2) * LANES]
            values = (
                jnp.where(lane < half, even, pltpu.roll(odd, half, 1)),
                jnp.where(lane < half, pltpu.roll(even, half, 1), odd),
            )
            block = chunk * group + member
            for drift, value in enumerate(values):
                o_ref[
                    outer,
                    pl.ds(block * SUBLANES + inner + drift, LANES, stride=SUBLANES * blocks),
                    :,
                ] = value
        return carry

    lax.fori_loop(0, pairs * chunks, multiply, 0)


def correlate_stage(arrived, halo, bands):
    devices, _, _, slots, lines, count = arrived.shape
    total = 2 * devices * slots
    drifts = 2 * bands.shape[0]
    groups = drifts // SUBLANES
    pad = SUBLANES
    flat = arrived.reshape(devices * 4 * slots * lines, count)
    height = count * total // LANES * SUBLANES
    out = pl.pallas_call(
        functools.partial(correlate_kernel, devices, slots, pad),
        grid=(lines,),
        in_specs=[
            pl.BlockSpec(flat.shape, lambda i: (0, 0), pipeline_mode=pl.Buffered(1)),
            pl.BlockSpec(halo.shape, lambda i: (0, 0)),
            pl.BlockSpec(bands.shape, lambda i: (0, 0, 0), pipeline_mode=pl.Buffered(1)),
        ],
        out_specs=pl.BlockSpec((groups, height, LANES), lambda i: (0, i, 0)),
        out_shape=jax.ShapeDtypeStruct((groups, lines * height, LANES), F32),
        scratch_shapes=[
            pltpu.VMEM((2 * SUBLANES * (total + pad), LANES), F32),
            pltpu.VMEM((2, LANES), F32),
            pltpu.VMEM((2 * total // LANES * LANES, 6 * LANES), BF16),
        ],
        compiler_params=pltpu.CompilerParams(vmem_limit_bytes=VMEM_LIMIT),
        name="correlate",
    )(flat, halo, bands)
    out = out.reshape(groups, lines * height // SUBLANES, SUBLANES, LANES)
    return jnp.swapaxes(out, 1, 2).reshape(drifts, lines * height // SUBLANES * LANES)


def halo_lines(arrived, taps):
    half = taps // 2
    devices, _, _, slots, lines, count = arrived.shape
    total = 2 * devices * slots
    first = arrived[:, 0, :, :, 0, 0]
    final = arrived[:, 1, :, :, lines - 1, count - 1]
    spread = lambda a: jnp.swapaxes(a, 0, 1).reshape(2, devices * slots)
    head = spread(first)[:, :half]
    tail = spread(final)[:, 1 : half + 1][:, ::-1]
    size = lax.axis_size(AXES)
    forward = [(i, i + 1) for i in range(size - 1)]
    backward = [(i + 1, i) for i in range(size - 1)]
    previous = lax.ppermute(tail, AXES, forward)
    following = lax.ppermute(head, AXES, backward)
    return jnp.concatenate(
        [
            jnp.pad(previous, ((0, 0), (0, LANES - half))),
            jnp.pad(following, ((0, 0), (half, LANES - 2 * half))),
        ],
        axis=0,
    )


def tap_kernels(templates, drift_template, drift_reach):
    taps = templates.shape[1] // 2
    selector = (drift_template[:, None] == iota(templates.shape[0])[None, :]).astype(F32)
    chosen = jnp.dot(
        selector, templates, precision=lax.Precision.HIGHEST, preferred_element_type=F32
    )
    index = iota(taps)[None, :]
    center = taps // 2
    inside = (
        (index >= center - drift_reach[:, None]) & (index < center + drift_reach[:, None])
    ).astype(F32)
    return chosen[:, :taps] * inside, chosen[:, taps:] * inside


def fits(shape, devices, drifts, taps):
    rows, cols = shape[1], shape[2]
    lines = devices * cols // LANES
    return (
        2 * LANES // devices == SUBLANES
        and lines // devices == SUBLANES
        and rows % (2 * devices * SUBLANES) == 0
        and drifts % SUBLANES == 0
        and 2 * taps == LANES
    )


def local(series, templates, drift_template, drift_reach):
    position = lax.axis_index(AXES)
    devices = lax.axis_size(AXES)
    rows, cols = series.shape[1], series.shape[2]
    taps = templates.shape[1] // 2
    if not fits(series.shape, devices, drift_template.shape[0], taps):
        return general_local(series, templates, drift_template, drift_reach)
    count = LANES
    width = devices * cols // count
    slots = rows // 2 // devices
    samples = 2 * rows * cols * devices
    bands = band_stage(*tap_kernels(templates, drift_template, drift_reach))
    columns = column_stage(series, position, width)
    columns = columns.reshape(devices, slots, 2 * width // LANES, SUBLANES, LANES)
    arrived = lax.all_to_all(columns, AXES, 0, 0, tiled=True)
    spectra = row_stage(arrived, position, rows, samples)
    arrived = lax.all_to_all(spectra, AXES, 0, 0, tiled=True)
    return correlate_stage(arrived, halo_lines(arrived, taps), bands)


def solution(mesh):
    return jax.shard_map(
        local,
        mesh=mesh,
        in_specs=(P(None, None, AXES), P(), P(), P()),
        out_specs=P(None, AXES),
        check_vma=False,
    )
```

```python
import functools
import math

import jax
import jax.numpy as jnp
from jax import lax
from jax.experimental import pallas as pl
from jax.experimental.pallas import tpu as pltpu
from jax.sharding import PartitionSpec as P


AXES = ("grp", "dev")
LANES = 128
SUBLANES = 8
VMEM_LIMIT = 60 * 1024 * 1024
PARTS = 2
F32 = jnp.float32
BF16 = jnp.bfloat16


def split(x):
    high = x.astype(BF16)
    return high, (x - high.astype(F32)).astype(BF16)


def split_xla(x):
    high = lax.reduce_precision(x, 8, 7)
    return high.astype(BF16), lax.reduce_precision(x - high, 8, 7).astype(BF16)


def phases(product, length):
    angles = (product % length).astype(F32) * (2.0 * math.pi / length)
    return jnp.cos(angles), jnp.sin(angles)


def iota(count):
    return jnp.arange(count, dtype=jnp.int32)


P1 = 32
P2 = 32
Q1 = 128
Q2 = 256
N = 67108864
M = 33554432
TAPS = 64
HIGHEST = lax.Precision.HIGHEST


def extended_2(block, sides, width):
    for axis, dim in sides:
        count = lax.axis_size(axis)
        forward = [(i, i + 1) for i in range(count - 1)]
        backward = [(target, source) for source, target in forward]
        low = lax.ppermute(
            lax.slice_in_dim(block, block.shape[dim] - width, None, axis=dim), axis, forward
        )
        high = lax.ppermute(lax.slice_in_dim(block, 0, width, axis=dim), axis, backward)
        block = jnp.concatenate([low, block, high], axis=dim)
    return block


def dft_table(length):
    indices = jnp.arange(length, dtype=jnp.int32)
    product = indices[:, None] * indices[None, :] % length
    angles = product.astype(jnp.float32) * (-2.0 * math.pi / length)
    return (jnp.cos(angles), jnp.sin(angles))


def twiddle(row_index, col_index, length):
    product = row_index[:, None] * col_index[None, :] % length
    angles = product.astype(jnp.float32) * (-2.0 * math.pi / length)
    return (jnp.cos(angles), jnp.sin(angles))


def complex_einsum(formula, left_pair, right_pair):
    left_real, left_imag = left_pair
    right_real, right_imag = right_pair
    real_part = jnp.einsum(formula, left_real, right_real, precision=HIGHEST) - jnp.einsum(
        formula, left_imag, right_imag, precision=HIGHEST
    )
    imag_part = jnp.einsum(formula, left_real, right_imag, precision=HIGHEST) + jnp.einsum(
        formula, left_imag, right_real, precision=HIGHEST
    )
    return (real_part, imag_part)


def complex_scale(values, factor):
    values_real, values_imag = values
    factor_real, factor_imag = factor
    return (
        values_real * factor_real - values_imag * factor_imag,
        values_real * factor_imag + values_imag * factor_real,
    )


def column_transform(series):
    col_count = series.shape[2]
    blocks = series.reshape(2, P1, P2, col_count)
    first_table = dft_table(P1)
    sectioned = (
        jnp.einsum("ja,eabc->ejbc", first_table[0], blocks, precision=HIGHEST),
        jnp.einsum("ja,eabc->ejbc", first_table[1], blocks, precision=HIGHEST),
    )
    inner_turn = twiddle(jnp.arange(P1, dtype=jnp.int32), jnp.arange(P2, dtype=jnp.int32), P1 * P2)
    sectioned = complex_scale(
        sectioned, (inner_turn[0][None, :, :, None], inner_turn[1][None, :, :, None])
    )
    sectioned = complex_einsum("kb,ejbc->ekjc", dft_table(P2), sectioned)
    return (
        sectioned[0].reshape(2, P1 * P2, col_count),
        sectioned[1].reshape(2, P1 * P2, col_count),
    )


def row_transform(values):
    parts_count, row_count = (values[0].shape[0], values[0].shape[1])
    shaped = (
        values[0].reshape(parts_count, row_count, Q1, Q2),
        values[1].reshape(parts_count, row_count, Q1, Q2),
    )
    sectioned = complex_einsum("ja,kbac->kbjc", dft_table(Q1), shaped)
    inner_turn = twiddle(jnp.arange(Q1, dtype=jnp.int32), jnp.arange(Q2, dtype=jnp.int32), Q1 * Q2)
    sectioned = complex_scale(sectioned, (inner_turn[0][None, None], inner_turn[1][None, None]))
    sectioned = complex_einsum("lc,kbjc->kblj", dft_table(Q2), sectioned)
    return (
        sectioned[0].reshape(parts_count, row_count, Q1 * Q2),
        sectioned[1].reshape(parts_count, row_count, Q1 * Q2),
    )


def combine_halves(even_part, odd_part, frequency):
    angles = frequency.astype(jnp.float32) * (-2.0 * math.pi / N)
    turned = complex_scale(odd_part, (jnp.cos(angles), jnp.sin(angles)))
    norm_scale = 1.0 / math.sqrt(N)
    return ((even_part[0] + turned[0]) * norm_scale, (even_part[1] + turned[1]) * norm_scale)


def to_rows(stacked):
    group_count = lax.axis_size("grp")
    member_count = lax.axis_size("dev")
    leading = stacked.shape[0]
    col_count = stacked.shape[2]
    row_count = stacked.shape[1] // (group_count * member_count)
    shaped = stacked.reshape(leading, group_count, member_count, row_count, 1, 1, col_count)
    arrived = lax.all_to_all(
        lax.all_to_all(shaped, "grp", split_axis=1, concat_axis=4, tiled=True),
        "dev",
        split_axis=2,
        concat_axis=5,
        tiled=True,
    )
    return arrived.reshape(leading, row_count, group_count * member_count * col_count)


def to_segments(stacked):
    group_count = lax.axis_size("grp")
    member_count = lax.axis_size("dev")
    leading = stacked.shape[0]
    row_count = stacked.shape[1]
    col_count = stacked.shape[2] // (group_count * member_count)
    shaped = stacked.reshape(leading, 1, 1, row_count, group_count, member_count, col_count)
    arrived = lax.all_to_all(
        lax.all_to_all(shaped, "grp", split_axis=4, concat_axis=1, tiled=True),
        "dev",
        split_axis=5,
        concat_axis=2,
        tiled=True,
    )
    gathered = arrived.reshape(leading, group_count * member_count * row_count, col_count)
    return jnp.swapaxes(gathered, 1, 2).reshape(
        leading, col_count * group_count * member_count * row_count
    )


def general_taps(templates, drift_template, drift_reach):
    template_count = templates.shape[0]
    selector = (
        drift_template[:, None] == jnp.arange(template_count, dtype=jnp.int32)[None, :]
    ).astype(jnp.float32)
    chosen = jnp.dot(selector, templates, precision=HIGHEST, preferred_element_type=jnp.float32)
    taps_index = jnp.arange(TAPS, dtype=jnp.int32)[None, :]
    center = TAPS // 2
    inside = (
        (taps_index >= center - drift_reach[:, None]) & (taps_index < center + drift_reach[:, None])
    ).astype(jnp.float32)
    return (chosen[:, :TAPS] * inside, chosen[:, TAPS:] * inside)


def general_banded(kernel_rows, window_width):
    lane_width = 128
    drift_count = kernel_rows.shape[0]
    padded = jnp.concatenate(
        [kernel_rows, jnp.zeros((drift_count, window_width + 1 - TAPS), jnp.float32)], axis=1
    )
    tiled_rows = jnp.tile(padded, (1, lane_width))[:, : lane_width * window_width]
    return jnp.swapaxes(tiled_rows.reshape(drift_count, lane_width, window_width), 1, 2)


def correlate(extended, kernels, segment_bins):
    lane_width = 128
    row_count = segment_bins // lane_width
    window_width = lane_width + TAPS
    head_rows = extended[:, :segment_bins].reshape(2, row_count, lane_width)
    rest_bins = jnp.concatenate(
        [extended[:, lane_width:], jnp.zeros((2, lane_width - TAPS), jnp.float32)], axis=1
    )
    tail_rows = rest_bins.reshape(2, row_count, lane_width)[:, :, :TAPS]
    windows = jnp.concatenate([head_rows, tail_rows], axis=2)
    flat_windows = jnp.concatenate([windows[0], windows[1]], axis=1)
    band_real = general_banded(kernels[0], window_width)
    band_imag = general_banded(kernels[1], window_width)
    matrices = jnp.concatenate(
        [
            jnp.concatenate([band_real, band_imag], axis=2),
            jnp.concatenate([-band_imag, band_real], axis=2),
        ],
        axis=1,
    )
    response = jnp.einsum(
        "rw,dwo->dro", flat_windows, matrices, precision=HIGHEST, preferred_element_type=jnp.float32
    )
    power_rows = (
        response[:, :, :lane_width] * response[:, :, :lane_width]
        + response[:, :, lane_width:] * response[:, :, lane_width:]
    )
    return power_rows.reshape(power_rows.shape[0], row_count * lane_width)


def general_local(series, templates, drift_template, drift_reach):
    position = lax.axis_index(("grp", "dev"))
    col_count = series.shape[2]
    row_total = P1 * P2
    row_frequency = jnp.arange(row_total, dtype=jnp.int32)
    columns = position * col_count + jnp.arange(col_count, dtype=jnp.int32)
    column_turn = twiddle(row_frequency, columns, M)
    section_real, section_imag = column_transform(series)
    turned = complex_scale(
        (section_real, section_imag), (column_turn[0][None], column_turn[1][None])
    )
    by_rows = to_rows(jnp.concatenate([turned[0], turned[1]], axis=0))
    spectrum = row_transform((by_rows[0:2], by_rows[2:4]))
    row_count = by_rows.shape[1]
    row_index = position * row_count + jnp.arange(row_count, dtype=jnp.int32)
    frequency = row_index[:, None] + row_total * jnp.arange(Q1 * Q2, dtype=jnp.int32)[None, :]
    whole_real, whole_imag = combine_halves(
        (spectrum[0][0], spectrum[1][0]), (spectrum[0][1], spectrum[1][1]), frequency
    )
    segment = to_segments(jnp.stack([whole_real, whole_imag]))
    segment_bins = segment.shape[1]
    kernels = general_taps(templates, drift_template, drift_reach)
    extended = extended_2(segment, ((("grp", "dev"), 1),), TAPS // 2)
    return correlate(extended, kernels, segment_bins)


def column_kernel(packed, *refs):
    inner = SUBLANES // 2
    x_refs, refs = refs[:inner], refs[inner:]
    near_re_ref, near_im_ref, far_re_ref, far_im_ref = refs[:4]
    base_re_ref, base_im_ref, step_re_ref, step_im_ref, o_ref, table, stage = refs[4:]
    slots = base_re_ref.shape[0]
    rows = x_refs[0].shape[1]
    span = slots + SUBLANES

    @pl.when(pl.program_id(0) == 0)
    def _():
        near_re = near_re_ref[...]
        near_im = near_im_ref[...]
        slot = lax.broadcasted_iota(jnp.int32, (slots, LANES), 0)
        lane = lax.broadcasted_iota(jnp.int32, (slots, LANES), 1)
        alternating = jnp.where(lane % 2 == 0, 1.0, -1.0).astype(F32)
        for block in range(rows // LANES):
            far_re = far_re_ref[:, block : block + 1]
            far_im = far_im_ref[:, block : block + 1]
            cos = near_re * far_re - near_im * far_im
            sin = near_re * far_im + near_im * far_re
            sin = jnp.where(slot == 0, alternating, -sin) if packed else -sin
            for part, value in enumerate((cos, sin)):
                high, low = split(value)
                lines = slice(part * slots, (part + 1) * slots)
                table[lines, block * LANES : (block + 1) * LANES] = high
                table[lines, rows + block * LANES : rows + (block + 1) * LANES] = low

    high, low = split(jnp.concatenate([r[0] for r in x_refs], axis=1))
    out = jnp.dot(
        table[...], jnp.concatenate([high, high], axis=0), preferred_element_type=F32
    ) + jnp.dot(table[:, :rows], low, preferred_element_type=F32)
    base_re = base_re_ref[...]
    base_im = base_im_ref[...]
    for block in range(inner):
        lanes = slice(block * LANES, (block + 1) * LANES)
        step_re = step_re_ref[0, :, block : block + 1]
        step_im = step_im_ref[0, :, block : block + 1]
        turn_re = base_re * step_re - base_im * step_im
        turn_im = base_re * step_im + base_im * step_re
        real = out[:slots, lanes]
        imag = out[slots:, lanes]
        stage[block * span : block * span + slots, :] = real * turn_re + imag * turn_im
        start = (inner + block) * span
        stage[start : start + slots, :] = imag * turn_re - real * turn_im
    for slot in range(slots):
        o_ref[slot, 0] = stage[pl.ds(slot, SUBLANES, stride=span), :]


def column_stage(series, position, width, part):
    rows, cols = series.shape[1], series.shape[2]
    slots = rows // 2 // PARTS
    inner = cols // width
    chunks = width // LANES
    samples = 2 * rows * cols * lax.axis_size(AXES)
    slot = part * slots + iota(slots)
    near_re, near_im = phases(slot[:, None] * iota(LANES)[None, :], rows)
    far_re, far_im = phases(slot[:, None] * (LANES * iota(rows // LANES))[None, :], rows)
    base_re, base_im = phases(slot[:, None] * (2 * iota(LANES))[None, :], samples)
    start = (
        2 * (position * cols + width * iota(inner)[None, None, :] + LANES * iota(chunks)[None, :, None])
        + iota(2)[:, None, None]
    ).reshape(2 * chunks * inner, 1)
    steps = [
        jnp.swapaxes(a.reshape(2 * chunks, inner, slots), 1, 2)
        for a in phases(start * slot[None, :], samples)
    ]
    small = pl.BlockSpec((1, slots, inner), lambda i: (i, 0, 0))
    whole = lambda a: pl.BlockSpec(a.shape, lambda i: (0, 0))
    column = lambda block: pl.BlockSpec(
        (1, rows, LANES), lambda i: (i // chunks, 0, block * chunks + i % chunks)
    )
    tables = (near_re, near_im, far_re, far_im, base_re, base_im)
    return pl.pallas_call(
        functools.partial(column_kernel, part == 0),
        grid=(2 * chunks,),
        in_specs=[column(block) for block in range(inner)]
        + [whole(table) for table in tables]
        + [small, small],
        out_specs=pl.BlockSpec((slots, 1, SUBLANES, LANES), lambda i: (0, i, 0, 0)),
        out_shape=jax.ShapeDtypeStruct((slots, 2 * chunks, SUBLANES, LANES), F32),
        scratch_shapes=[
            pltpu.VMEM((2 * slots, 2 * rows), BF16),
            pltpu.VMEM(((SUBLANES + 1) * (slots + SUBLANES), LANES), F32),
        ],
        compiler_params=pltpu.CompilerParams(vmem_limit_bytes=VMEM_LIMIT),
        cost_estimate=pl.CostEstimate(
            flops=24 * slots * rows * cols, transcendentals=0, bytes_accessed=12 * rows * cols
        ),
        name="columns",
    )(*[series] * inner, *tables, *steps)


def row_kernel(variant_ref, x_ref, first_ref, turn_ref, second_ref, *o_refs):
    depth = first_ref.shape[2] // 3
    count, width = turn_ref.shape[3], turn_ref.shape[4]
    x = [x_ref[:, 0, i].reshape(depth, LANES) for i in range(width // LANES)]
    high, low = split(jnp.concatenate(x, axis=1))
    out = jnp.dot(
        first_ref[0], jnp.concatenate([high, high, low], axis=0), preferred_element_type=F32
    )
    pieces = []
    for side in range(2):
        real = out[2 * side * count : (2 * side + 1) * count]
        imag = out[(2 * side + 1) * count : (2 * side + 2) * count]
        turn_re = turn_ref[0, side, 0]
        turn_im = turn_ref[0, side, 1]
        turned = jnp.concatenate(
            [real * turn_re + imag * turn_im, imag * turn_re - real * turn_im], axis=1
        )
        high, low = split(turned)
        pieces.append(jnp.concatenate([high, high, low], axis=1))
    result = lax.dot_general(
        second_ref[...],
        jnp.concatenate(pieces, axis=0),
        (((1,), (1,)), ((), ())),
        preferred_element_type=F32,
    )
    height = result.shape[0] // len(o_refs)
    for index, o_ref in enumerate(o_refs):
        for side in range(2):
            block = result[
                index * height : (index + 1) * height, side * count : (side + 1) * count
            ]
            o_ref[:, side, 0] = block.reshape(height // SUBLANES, SUBLANES, count)


def row_tables(devices, chunks, sublanes, samples):
    width = chunks * LANES
    inner = sublanes // 2
    count = devices * inner
    lines = width // 2
    freq = iota(count)[:, None]
    order = (inner * iota(devices)[:, None] + iota(inner)[None, :]).reshape(1, devices, inner)
    fc, fs = phases(freq[:, :, None] * order, count)
    bc, bs = phases((freq[:, :, None] + 1) * order, count)
    hc, hs = phases((2 * freq[:, :, None] + 1) * order, 2 * count)
    zero = jnp.zeros_like(fc)
    pack = lambda on_re, on_im: jnp.stack([on_re, on_im], axis=2).reshape(count, devices * sublanes)
    usual = jnp.concatenate([pack(fc, fs), pack(-fs, fc), pack(bc, -bs), pack(-bs, -bc)], axis=0)
    special = jnp.concatenate(
        [pack(fc, zero), pack(-fs, zero), pack(zero, hc), pack(zero, -hs)], axis=0
    )
    high, low = split_xla(jnp.stack([usual, special]))
    first = jnp.concatenate([high, low, high], axis=2)
    beta = (2 * iota(lines)[None, :] + iota(2)[:, None]).reshape(1, width)
    length = count * width
    turn_a = jnp.stack(phases(freq * beta, length))
    turn_b = jnp.stack(phases((freq + 1) * beta, length))
    turn_c = jnp.stack(phases((2 * freq + 1) * beta, 2 * length))
    turn = jnp.stack([jnp.stack([turn_a, turn_b]), jnp.stack([turn_a, turn_c])])
    inside = SUBLANES // 2
    line = (
        SUBLANES * iota(devices)[None, :, None]
        + inside * iota(PARTS)[:, None, None]
        + iota(inside)[None, None, :]
    )
    gc, gs = [
        a.reshape(PARTS, devices, inside, width)
        for a in phases(line.reshape(lines, 1) * beta, width)
    ]
    second = jnp.stack(
        [jnp.concatenate([gc, gs], axis=3), jnp.concatenate([-gs, gc], axis=3)], axis=2
    ).reshape(2 * lines, 2 * width) * (1.0 / math.sqrt(samples))
    high, low = split_xla(second)
    second = jnp.concatenate([high, low, high], axis=1)
    return first, turn, second


def row_stage(arrived, tables, position, part):
    devices, slots, chunks, sublanes, _ = arrived.shape
    first, turn, second = tables
    count = turn.shape[4 - 1]
    variant = jnp.where((iota(slots) == 0) & (position == 0), 1, 0).astype(jnp.int32)
    if part > 0:
        variant = jnp.zeros((slots,), jnp.int32)
    blocks = second.shape[0] // PARTS // SUBLANES
    shape = (blocks, 2, slots, SUBLANES, count)
    return pl.pallas_call(
        row_kernel,
        grid_spec=pltpu.PrefetchScalarGridSpec(
            num_scalar_prefetch=1,
            grid=(slots,),
            in_specs=[
                pl.BlockSpec((devices, 1, chunks, sublanes, LANES), lambda i, v: (0, i, 0, 0, 0)),
                pl.BlockSpec((1,) + first.shape[1:], lambda i, v: (v[i], 0, 0)),
                pl.BlockSpec((1,) + turn.shape[1:], lambda i, v: (v[i], 0, 0, 0, 0)),
                pl.BlockSpec(second.shape, lambda i, v: (0, 0)),
            ],
            out_specs=[
                pl.BlockSpec((blocks, 2, 1, SUBLANES, count), lambda i, v: (0, 0, i, 0, 0))
                for _ in range(PARTS)
            ],
        ),
        out_shape=[jax.ShapeDtypeStruct(shape, F32) for _ in range(PARTS)],
        compiler_params=pltpu.CompilerParams(vmem_limit_bytes=VMEM_LIMIT),
        cost_estimate=pl.CostEstimate(
            flops=slots * 2 * (first.shape[1] * first.shape[2] * chunks * LANES + 2 * count * second.size),
            transcendentals=0,
            bytes_accessed=8 * arrived.size,
        ),
        name="rows",
    )(variant, arrived, first, turn, second)


def band_kernel(taps_ref, o_ref):
    half = LANES // 2
    banded = []
    for drift in range(2):
        for part in range(2):
            line = jnp.broadcast_to(taps_ref[0, 2 * drift + part : 2 * drift + part + 1, :], (half, LANES))
            banded.append(pltpu.roll(line, 0, 1, stride=1, stride_axis=0))
    re = jnp.concatenate([banded[0], banded[2]], axis=0)
    im = jnp.concatenate([banded[1], banded[3]], axis=0)
    lines = jnp.concatenate(
        [jnp.concatenate([re, -im], axis=1), jnp.concatenate([im, re], axis=1)], axis=0
    )
    high, low = split(jnp.transpose(lines))
    o_ref[0] = jnp.concatenate([high, low, high], axis=0)


def band_stage(kernel_re, kernel_im):
    drifts, taps = kernel_re.shape
    lines = jnp.stack([kernel_re, kernel_im], axis=1)
    lines = jnp.pad(lines, ((0, 0), (0, 0), (0, LANES - taps))).reshape(drifts // 2, 4, LANES)
    return pl.pallas_call(
        band_kernel,
        grid=(drifts // 2,),
        in_specs=[pl.BlockSpec((1, 4, LANES), lambda i: (i, 0, 0))],
        out_specs=pl.BlockSpec((1, 6 * LANES, 2 * LANES), lambda i: (i, 0, 0)),
        out_shape=jax.ShapeDtypeStruct((drifts // 2, 6 * LANES, 2 * LANES), BF16),
        name="bands",
    )(lines)


def correlate_kernel(
    devices, slots, pad, inputs, *refs
):
    x_refs, (halo_ref, band_ref) = refs[:inputs], refs[inputs : inputs + 2]
    o_ref, table, last, lhs, stage_a, stage_b = refs[-6:]
    step = pl.program_id(0)
    steps = pl.num_programs(0)
    inside = SUBLANES // 2
    total = 2 * PARTS * devices * slots
    pitch = total + pad
    half = LANES // 2
    taps_half = half // 2

    @pl.when(step == 0)
    def _():
        def source(s, carry):
            for part in range(PARTS):
                for side in range(2):
                    for slot in range(slots):
                        x_ref = x_refs[min(part, inputs - 1)]
                        tiles = x_ref.shape[0] // devices // SUBLANES
                        place = (part * 2 + side if inputs < PARTS else side) * slots + slot
                        start = (s * tiles + place) * SUBLANES
                        tile = x_ref[pl.ds(pl.multiple_of(start, SUBLANES), SUBLANES), :]
                        row = (part * devices + s) * slots + slot
                        if side == 1:
                            row = total - row
                            if slot == 0 and part == 0:
                                row = jnp.where(s == 0, total // 2, row)
                        table[pl.ds(row, SUBLANES, stride=pitch), :] = tile
            return carry

        lax.fori_loop(0, devices, source, 0)
        last[...] = halo_ref[0:2, :]

    lane = lax.broadcasted_iota(jnp.int32, (LANES, LANES), 1)
    row_id = lax.broadcasted_iota(jnp.int32, (LANES, LANES), 0)
    blocks = total // LANES

    def turned(part, line, block):
        start = pl.multiple_of((part * inside + line) * pitch + block * LANES, SUBLANES)
        flat = jnp.transpose(table[pl.ds(start, LANES), :])
        return pltpu.roll(flat, taps_half, 1)

    next_line = jnp.minimum(step + 1, steps - 1)
    for part in range(2):
        rolled = [turned(part, step, block) for block in range(blocks)]
        follow = turned(part, next_line, 0)[0:1, :]
        follow = jnp.where(step == steps - 1, halo_ref[2 + part : 3 + part, :], follow)
        before = jnp.where(row_id == 0, last[part : part + 1, :], pltpu.roll(rolled[-1], 1, 0))
        after = jnp.where(row_id == LANES - 1, follow, pltpu.roll(rolled[0], LANES - 1, 0))
        last[part : part + 1, :] = rolled[-1][LANES - 1 : LANES, :]
        ext = []
        for block in range(blocks + 1):
            left = before if block == 0 else rolled[block - 1]
            right = after if block == blocks else rolled[block]
            ext.append(jnp.where(lane < taps_half, left, right))
        for block in range(blocks):
            odd = jnp.where(
                lane < half, pltpu.roll(ext[block], half, 1), pltpu.roll(ext[block + 1], half, 1)
            )
            for parity, window in enumerate((ext[block], odd)):
                high, low = split(window)
                rows = pl.ds((2 * block + parity) * LANES, LANES)
                lhs[rows, part * LANES : (part + 1) * LANES] = high
                lhs[rows, (2 + part) * LANES : (3 + part) * LANES] = high
                lhs[rows, (4 + part) * LANES : (5 + part) * LANES] = low

    group = 2
    chunks = blocks // group
    drifts = SUBLANES
    span = LANES + SUBLANES

    def multiply(chunk, outer, target):
        rows = pl.ds(pl.multiple_of(chunk * group * 2 * LANES, LANES), group * 2 * LANES)
        windows = lhs[rows, :]
        for pair in range(drifts // 2):
            out = jnp.dot(
                windows, band_ref[outer * drifts // 2 + pair], preferred_element_type=F32
            )
            power = out[:, :LANES] * out[:, :LANES] + out[:, LANES:] * out[:, LANES:]
            for member in range(group):
                even = power[member * 2 * LANES : (member * 2 + 1) * LANES]
                odd = power[(member * 2 + 1) * LANES : (member * 2 + 2) * LANES]
                start = (member * drifts + 2 * pair) * span
                target[start : start + LANES, :] = jnp.where(lane < half, even, pltpu.roll(odd, half, 1))
                start += span
                target[start : start + LANES, :] = jnp.where(lane < half, pltpu.roll(even, half, 1), odd)

    def emit(chunk, outer, origin):
        for member in range(group):
            for line in range(LANES):
                value = origin[pl.ds(member * drifts * span + line, drifts, stride=span), :]
                start = (line * blocks + member + chunk * group) * SUBLANES
                o_ref[outer, pl.ds(pl.multiple_of(start, SUBLANES), SUBLANES), :] = value

    groups = o_ref.shape[0]
    stages = (stage_a, stage_b)

    def body(chunk, carry):
        for outer in range(groups):
            multiply(chunk, outer, stages[outer % 2])
            if outer == 0:
                emit(jnp.maximum(chunk - 1, 0), groups - 1, stages[(groups - 1) % 2])
            else:
                emit(chunk, outer - 1, stages[(outer - 1) % 2])
        return carry

    lax.fori_loop(0, chunks, body, 0)
    emit(chunks - 1, groups - 1, stages[(groups - 1) % 2])


def correlate_stage(arrived, halo, bands, part, earlier, slots):
    devices, _, _, count = arrived[0].shape
    total = 2 * PARTS * devices * slots
    drifts = 2 * bands.shape[0]
    groups = drifts // SUBLANES
    pad = SUBLANES
    inside = SUBLANES // 2
    flat = [a.reshape(-1, count) for a in arrived]
    height = count * total // LANES * SUBLANES
    resident = lambda shape: pl.BlockSpec(
        shape, lambda i: (0,) * len(shape), pipeline_mode=pl.Buffered(1)
    )
    extra = [] if earlier is None else [earlier]
    return pl.pallas_call(
        functools.partial(correlate_kernel, devices, slots, pad, len(flat)),
        grid=(inside,),
        in_specs=[resident(a.shape) for a in flat]
        + [resident(halo.shape), resident(bands.shape)]
        + [pl.BlockSpec(memory_space=pl.ANY) for _ in extra],
        out_specs=pl.BlockSpec((groups, height, LANES), lambda i: (0, part * inside + i, 0)),
        out_shape=jax.ShapeDtypeStruct((groups, PARTS * inside * height, LANES), F32),
        input_output_aliases={} if earlier is None else {len(flat) + 2: 0},
        scratch_shapes=[
            pltpu.VMEM(((SUBLANES + 1) * (total + pad), LANES), F32),
            pltpu.VMEM((2, LANES), F32),
            pltpu.VMEM((2 * total // LANES * LANES, 6 * LANES), BF16),
            pltpu.VMEM(((2 * SUBLANES + 1) * (LANES + SUBLANES), LANES), F32),
            pltpu.VMEM(((2 * SUBLANES + 1) * (LANES + SUBLANES), LANES), F32),
        ],
        compiler_params=pltpu.CompilerParams(vmem_limit_bytes=VMEM_LIMIT),
        cost_estimate=pl.CostEstimate(
            flops=inside * 12 * bands.shape[0] * total * count * LANES * 2 // 8,
            transcendentals=0,
            bytes_accessed=groups * inside * height * LANES * 4,
        ),
        name="correlate",
    )(*flat, halo, bands, *extra)


def edge_lines(spectra):
    low, high = spectra
    devices, _, slots, sublanes, count = low.shape
    inside = sublanes // 2
    first = lambda a: a[:, 0, :, ::inside, 0]
    final = lambda a: a[:, 1, :, inside - 1 :: inside, count - 1]
    blank = jnp.zeros_like(first(low)[:1])
    edges = jnp.stack(
        [
            jnp.concatenate([blank, final(high)[:-1]]),
            first(high),
            final(low),
            jnp.concatenate([first(low)[1:], blank]),
        ],
        axis=1,
    )
    edges = jnp.moveaxis(edges, 3, 2).reshape(devices, 1, 8, slots)
    return jnp.pad(edges, ((0, 0), (0, 0), (0, 0), (0, count - slots)))


def halo_lines(edges, slots, taps):
    half = taps // 2
    devices = edges.shape[0]
    lines = jnp.moveaxis(edges[:, :, :slots].reshape(devices, 4, 2, slots), 0, 2)
    lines = lines.reshape(4, 2, devices * slots)
    tail = lambda a: jnp.pad(a[:, half:0:-1], ((0, 0), (0, LANES - half)))
    head = lambda a: jnp.pad(a[:, :half], ((0, 0), (half, LANES - 2 * half)))
    return [
        jnp.concatenate([tail(lines[2 * part]), head(lines[2 * part + 1])], axis=0)
        for part in range(PARTS)
    ]


def tap_kernels(templates, drift_template, drift_reach):
    taps = templates.shape[1] // 2
    selector = (drift_template[:, None] == iota(templates.shape[0])[None, :]).astype(F32)
    chosen = jnp.dot(
        selector, templates, precision=lax.Precision.HIGHEST, preferred_element_type=F32
    )
    index = iota(taps)[None, :]
    center = taps // 2
    inside = (
        (index >= center - drift_reach[:, None]) & (index < center + drift_reach[:, None])
    ).astype(F32)
    return chosen[:, :taps] * inside, chosen[:, taps:] * inside


def fits(shape, devices, drifts, taps):
    rows, cols = shape[1], shape[2]
    lines = devices * cols // LANES
    return (
        2 * LANES // devices == SUBLANES
        and lines // devices == SUBLANES
        and rows % (2 * devices * SUBLANES) == 0
        and drifts % SUBLANES == 0
        and 2 * taps == LANES
    )


def local(series, templates, drift_template, drift_reach):
    position = lax.axis_index(AXES)
    devices = lax.axis_size(AXES)
    rows, cols = series.shape[1], series.shape[2]
    taps = templates.shape[1] // 2
    if not fits(series.shape, devices, drift_template.shape[0], taps):
        return general_local(series, templates, drift_template, drift_reach)
    width = devices * cols // LANES
    slots = rows // 2 // devices // PARTS
    samples = 2 * rows * cols * devices
    chunks = 2 * width // LANES
    arrived = []
    swap = lambda value: lax.all_to_all(value, AXES, 0, 0, tiled=True)
    tables = row_tables(devices, chunks, SUBLANES, samples)
    bands = band_stage(*tap_kernels(templates, drift_template, drift_reach))
    for part in range(PARTS):
        columns = column_stage(series, position, width, part)
        columns = columns.reshape(devices, slots, chunks, SUBLANES, LANES)
        if part == PARTS - 1:
            columns, tables, bands = lax.optimization_barrier((columns, tables, bands))
        arrived.append(swap(columns))
    pieces = []
    for part in range(PARTS):
        spectra = row_stage(arrived[part], tables, position, part)
        tiles = [a.reshape(devices, 2 * slots, SUBLANES, LANES) for a in spectra]
        if part == 0:
            tiles[0] = jnp.concatenate([tiles[0], edge_lines(spectra)], axis=1)
        pieces.append(tiles)
    first = swap(pieces[0][0])
    second = swap(pieces[1][0])
    rest = swap(jnp.concatenate([pieces[0][1], pieces[1][1]], axis=1))
    halos = halo_lines(first[:, 2 * slots], slots, taps)
    out = correlate_stage([first, second], halos[0], bands, 0, None, slots)
    out = correlate_stage([rest], halos[1], bands, 1, out, slots)
    groups = out.shape[0]
    out = out.reshape(groups, -1, SUBLANES, LANES)
    return jnp.swapaxes(out, 1, 2).reshape(groups * SUBLANES, -1)


def solution(mesh):
    return jax.shard_map(
        local,
        mesh=mesh,
        in_specs=(P(None, None, AXES), P(), P(), P()),
        out_specs=P(None, AXES),
        check_vma=False,
    )
```

```python
import functools
import math

import jax
import jax.numpy as jnp
from jax import lax
from jax.experimental import pallas as pl
from jax.experimental.pallas import tpu as pltpu
from jax.sharding import PartitionSpec as P


AXES = ("grp", "dev")
LANES = 128
SUBLANES = 8
VMEM_LIMIT = 60 * 1024 * 1024
PARTS = 2
SHARES = (1, 3)
F32 = jnp.float32
BF16 = jnp.bfloat16


def split(x):
    high = x.astype(BF16)
    return high, (x - high.astype(F32)).astype(BF16)


def split_xla(x):
    high = lax.reduce_precision(x, 8, 7)
    return high.astype(BF16), lax.reduce_precision(x - high, 8, 7).astype(BF16)


def phases(product, length):
    angles = (product % length).astype(F32) * (2.0 * math.pi / length)
    return jnp.cos(angles), jnp.sin(angles)


def iota(count):
    return jnp.arange(count, dtype=jnp.int32)


P1 = 32
P2 = 32
Q1 = 128
Q2 = 256
N = 67108864
M = 33554432
TAPS = 64
HIGHEST = lax.Precision.HIGHEST


def extended_2(block, sides, width):
    for axis, dim in sides:
        count = lax.axis_size(axis)
        forward = [(i, i + 1) for i in range(count - 1)]
        backward = [(target, source) for source, target in forward]
        low = lax.ppermute(
            lax.slice_in_dim(block, block.shape[dim] - width, None, axis=dim), axis, forward
        )
        high = lax.ppermute(lax.slice_in_dim(block, 0, width, axis=dim), axis, backward)
        block = jnp.concatenate([low, block, high], axis=dim)
    return block


def dft_table(length):
    indices = jnp.arange(length, dtype=jnp.int32)
    product = indices[:, None] * indices[None, :] % length
    angles = product.astype(jnp.float32) * (-2.0 * math.pi / length)
    return (jnp.cos(angles), jnp.sin(angles))


def twiddle(row_index, col_index, length):
    product = row_index[:, None] * col_index[None, :] % length
    angles = product.astype(jnp.float32) * (-2.0 * math.pi / length)
    return (jnp.cos(angles), jnp.sin(angles))


def complex_einsum(formula, left_pair, right_pair):
    left_real, left_imag = left_pair
    right_real, right_imag = right_pair
    real_part = jnp.einsum(formula, left_real, right_real, precision=HIGHEST) - jnp.einsum(
        formula, left_imag, right_imag, precision=HIGHEST
    )
    imag_part = jnp.einsum(formula, left_real, right_imag, precision=HIGHEST) + jnp.einsum(
        formula, left_imag, right_real, precision=HIGHEST
    )
    return (real_part, imag_part)


def complex_scale(values, factor):
    values_real, values_imag = values
    factor_real, factor_imag = factor
    return (
        values_real * factor_real - values_imag * factor_imag,
        values_real * factor_imag + values_imag * factor_real,
    )


def column_transform(series):
    col_count = series.shape[2]
    blocks = series.reshape(2, P1, P2, col_count)
    first_table = dft_table(P1)
    sectioned = (
        jnp.einsum("ja,eabc->ejbc", first_table[0], blocks, precision=HIGHEST),
        jnp.einsum("ja,eabc->ejbc", first_table[1], blocks, precision=HIGHEST),
    )
    inner_turn = twiddle(jnp.arange(P1, dtype=jnp.int32), jnp.arange(P2, dtype=jnp.int32), P1 * P2)
    sectioned = complex_scale(
        sectioned, (inner_turn[0][None, :, :, None], inner_turn[1][None, :, :, None])
    )
    sectioned = complex_einsum("kb,ejbc->ekjc", dft_table(P2), sectioned)
    return (
        sectioned[0].reshape(2, P1 * P2, col_count),
        sectioned[1].reshape(2, P1 * P2, col_count),
    )


def row_transform(values):
    parts_count, row_count = (values[0].shape[0], values[0].shape[1])
    shaped = (
        values[0].reshape(parts_count, row_count, Q1, Q2),
        values[1].reshape(parts_count, row_count, Q1, Q2),
    )
    sectioned = complex_einsum("ja,kbac->kbjc", dft_table(Q1), shaped)
    inner_turn = twiddle(jnp.arange(Q1, dtype=jnp.int32), jnp.arange(Q2, dtype=jnp.int32), Q1 * Q2)
    sectioned = complex_scale(sectioned, (inner_turn[0][None, None], inner_turn[1][None, None]))
    sectioned = complex_einsum("lc,kbjc->kblj", dft_table(Q2), sectioned)
    return (
        sectioned[0].reshape(parts_count, row_count, Q1 * Q2),
        sectioned[1].reshape(parts_count, row_count, Q1 * Q2),
    )


def combine_halves(even_part, odd_part, frequency):
    angles = frequency.astype(jnp.float32) * (-2.0 * math.pi / N)
    turned = complex_scale(odd_part, (jnp.cos(angles), jnp.sin(angles)))
    norm_scale = 1.0 / math.sqrt(N)
    return ((even_part[0] + turned[0]) * norm_scale, (even_part[1] + turned[1]) * norm_scale)


def to_rows(stacked):
    group_count = lax.axis_size("grp")
    member_count = lax.axis_size("dev")
    leading = stacked.shape[0]
    col_count = stacked.shape[2]
    row_count = stacked.shape[1] // (group_count * member_count)
    shaped = stacked.reshape(leading, group_count, member_count, row_count, 1, 1, col_count)
    arrived = lax.all_to_all(
        lax.all_to_all(shaped, "grp", split_axis=1, concat_axis=4, tiled=True),
        "dev",
        split_axis=2,
        concat_axis=5,
        tiled=True,
    )
    return arrived.reshape(leading, row_count, group_count * member_count * col_count)


def to_segments(stacked):
    group_count = lax.axis_size("grp")
    member_count = lax.axis_size("dev")
    leading = stacked.shape[0]
    row_count = stacked.shape[1]
    col_count = stacked.shape[2] // (group_count * member_count)
    shaped = stacked.reshape(leading, 1, 1, row_count, group_count, member_count, col_count)
    arrived = lax.all_to_all(
        lax.all_to_all(shaped, "grp", split_axis=4, concat_axis=1, tiled=True),
        "dev",
        split_axis=5,
        concat_axis=2,
        tiled=True,
    )
    gathered = arrived.reshape(leading, group_count * member_count * row_count, col_count)
    return jnp.swapaxes(gathered, 1, 2).reshape(
        leading, col_count * group_count * member_count * row_count
    )


def general_taps(templates, drift_template, drift_reach):
    template_count = templates.shape[0]
    selector = (
        drift_template[:, None] == jnp.arange(template_count, dtype=jnp.int32)[None, :]
    ).astype(jnp.float32)
    chosen = jnp.dot(selector, templates, precision=HIGHEST, preferred_element_type=jnp.float32)
    taps_index = jnp.arange(TAPS, dtype=jnp.int32)[None, :]
    center = TAPS // 2
    inside = (
        (taps_index >= center - drift_reach[:, None]) & (taps_index < center + drift_reach[:, None])
    ).astype(jnp.float32)
    return (chosen[:, :TAPS] * inside, chosen[:, TAPS:] * inside)


def general_banded(kernel_rows, window_width):
    lane_width = 128
    drift_count = kernel_rows.shape[0]
    padded = jnp.concatenate(
        [kernel_rows, jnp.zeros((drift_count, window_width + 1 - TAPS), jnp.float32)], axis=1
    )
    tiled_rows = jnp.tile(padded, (1, lane_width))[:, : lane_width * window_width]
    return jnp.swapaxes(tiled_rows.reshape(drift_count, lane_width, window_width), 1, 2)


def correlate(extended, kernels, segment_bins):
    lane_width = 128
    row_count = segment_bins // lane_width
    window_width = lane_width + TAPS
    head_rows = extended[:, :segment_bins].reshape(2, row_count, lane_width)
    rest_bins = jnp.concatenate(
        [extended[:, lane_width:], jnp.zeros((2, lane_width - TAPS), jnp.float32)], axis=1
    )
    tail_rows = rest_bins.reshape(2, row_count, lane_width)[:, :, :TAPS]
    windows = jnp.concatenate([head_rows, tail_rows], axis=2)
    flat_windows = jnp.concatenate([windows[0], windows[1]], axis=1)
    band_real = general_banded(kernels[0], window_width)
    band_imag = general_banded(kernels[1], window_width)
    matrices = jnp.concatenate(
        [
            jnp.concatenate([band_real, band_imag], axis=2),
            jnp.concatenate([-band_imag, band_real], axis=2),
        ],
        axis=1,
    )
    response = jnp.einsum(
        "rw,dwo->dro", flat_windows, matrices, precision=HIGHEST, preferred_element_type=jnp.float32
    )
    power_rows = (
        response[:, :, :lane_width] * response[:, :, :lane_width]
        + response[:, :, lane_width:] * response[:, :, lane_width:]
    )
    return power_rows.reshape(power_rows.shape[0], row_count * lane_width)


def general_local(series, templates, drift_template, drift_reach):
    position = lax.axis_index(("grp", "dev"))
    col_count = series.shape[2]
    row_total = P1 * P2
    row_frequency = jnp.arange(row_total, dtype=jnp.int32)
    columns = position * col_count + jnp.arange(col_count, dtype=jnp.int32)
    column_turn = twiddle(row_frequency, columns, M)
    section_real, section_imag = column_transform(series)
    turned = complex_scale(
        (section_real, section_imag), (column_turn[0][None], column_turn[1][None])
    )
    by_rows = to_rows(jnp.concatenate([turned[0], turned[1]], axis=0))
    spectrum = row_transform((by_rows[0:2], by_rows[2:4]))
    row_count = by_rows.shape[1]
    row_index = position * row_count + jnp.arange(row_count, dtype=jnp.int32)
    frequency = row_index[:, None] + row_total * jnp.arange(Q1 * Q2, dtype=jnp.int32)[None, :]
    whole_real, whole_imag = combine_halves(
        (spectrum[0][0], spectrum[1][0]), (spectrum[0][1], spectrum[1][1]), frequency
    )
    segment = to_segments(jnp.stack([whole_real, whole_imag]))
    segment_bins = segment.shape[1]
    kernels = general_taps(templates, drift_template, drift_reach)
    extended = extended_2(segment, ((("grp", "dev"), 1),), TAPS // 2)
    return correlate(extended, kernels, segment_bins)


def column_kernel(packed, *refs):
    inner = SUBLANES // 2
    x_refs, refs = refs[:inner], refs[inner:]
    near_re_ref, near_im_ref, far_re_ref, far_im_ref = refs[:4]
    base_re_ref, base_im_ref, step_re_ref, step_im_ref, o_ref, table, stage = refs[4:]
    slots = base_re_ref.shape[0]
    rows = x_refs[0].shape[1]
    span = slots + SUBLANES

    @pl.when(pl.program_id(0) == 0)
    def _():
        near_re = near_re_ref[...]
        near_im = near_im_ref[...]
        slot = lax.broadcasted_iota(jnp.int32, (slots, LANES), 0)
        lane = lax.broadcasted_iota(jnp.int32, (slots, LANES), 1)
        alternating = jnp.where(lane % 2 == 0, 1.0, -1.0).astype(F32)
        for block in range(rows // LANES):
            far_re = far_re_ref[:, block : block + 1]
            far_im = far_im_ref[:, block : block + 1]
            cos = near_re * far_re - near_im * far_im
            sin = near_re * far_im + near_im * far_re
            sin = jnp.where(slot == 0, alternating, -sin) if packed else -sin
            for part, value in enumerate((cos, sin)):
                high, low = split(value)
                lines = slice(part * slots, (part + 1) * slots)
                table[lines, block * LANES : (block + 1) * LANES] = high
                table[lines, rows + block * LANES : rows + (block + 1) * LANES] = low

    high, low = split(jnp.concatenate([r[0] for r in x_refs], axis=1))
    out = jnp.dot(
        table[...], jnp.concatenate([high, high], axis=0), preferred_element_type=F32
    ) + jnp.dot(table[:, :rows], low, preferred_element_type=F32)
    base_re = base_re_ref[...]
    base_im = base_im_ref[...]
    for block in range(inner):
        lanes = slice(block * LANES, (block + 1) * LANES)
        step_re = step_re_ref[0, :, block : block + 1]
        step_im = step_im_ref[0, :, block : block + 1]
        turn_re = base_re * step_re - base_im * step_im
        turn_im = base_re * step_im + base_im * step_re
        real = out[:slots, lanes]
        imag = out[slots:, lanes]
        stage[block * span : block * span + slots, :] = real * turn_re + imag * turn_im
        start = (inner + block) * span
        stage[start : start + slots, :] = imag * turn_re - real * turn_im
    for slot in range(slots):
        o_ref[slot, 0] = stage[pl.ds(slot, SUBLANES, stride=span), :]


def column_stage(series, position, width, first_slot, slots):
    rows, cols = series.shape[1], series.shape[2]
    inner = cols // width
    chunks = width // LANES
    samples = 2 * rows * cols * lax.axis_size(AXES)
    slot = first_slot + iota(slots)
    near_re, near_im = phases(slot[:, None] * iota(LANES)[None, :], rows)
    far_re, far_im = phases(slot[:, None] * (LANES * iota(rows // LANES))[None, :], rows)
    base_re, base_im = phases(slot[:, None] * (2 * iota(LANES))[None, :], samples)
    start = (
        2 * (position * cols + width * iota(inner)[None, None, :] + LANES * iota(chunks)[None, :, None])
        + iota(2)[:, None, None]
    ).reshape(2 * chunks * inner, 1)
    steps = [
        jnp.swapaxes(a.reshape(2 * chunks, inner, slots), 1, 2)
        for a in phases(start * slot[None, :], samples)
    ]
    small = pl.BlockSpec((1, slots, inner), lambda i: (i, 0, 0))
    whole = lambda a: pl.BlockSpec(a.shape, lambda i: (0, 0))
    column = lambda block: pl.BlockSpec(
        (1, rows, LANES), lambda i: (i // chunks, 0, block * chunks + i % chunks)
    )
    tables = (near_re, near_im, far_re, far_im, base_re, base_im)
    return pl.pallas_call(
        functools.partial(column_kernel, first_slot == 0),
        grid=(2 * chunks,),
        in_specs=[column(block) for block in range(inner)]
        + [whole(table) for table in tables]
        + [small, small],
        out_specs=pl.BlockSpec((slots, 1, SUBLANES, LANES), lambda i: (0, i, 0, 0)),
        out_shape=jax.ShapeDtypeStruct((slots, 2 * chunks, SUBLANES, LANES), F32),
        scratch_shapes=[
            pltpu.VMEM((2 * slots, 2 * rows), BF16),
            pltpu.VMEM(((SUBLANES + 1) * (slots + SUBLANES), LANES), F32),
        ],
        compiler_params=pltpu.CompilerParams(vmem_limit_bytes=VMEM_LIMIT),
        cost_estimate=pl.CostEstimate(
            flops=24 * slots * rows * cols, transcendentals=0, bytes_accessed=12 * rows * cols
        ),
        name="columns",
    )(*[series] * inner, *tables, *steps)


def row_kernel(variant_ref, x_ref, first_ref, turn_ref, second_ref, *o_refs):
    depth = first_ref.shape[2] // 3
    count, width = turn_ref.shape[3], turn_ref.shape[4]
    x = [x_ref[:, 0, i].reshape(depth, LANES) for i in range(width // LANES)]
    high, low = split(jnp.concatenate(x, axis=1))
    out = jnp.dot(
        first_ref[0], jnp.concatenate([high, high, low], axis=0), preferred_element_type=F32
    )
    pieces = []
    for side in range(2):
        real = out[2 * side * count : (2 * side + 1) * count]
        imag = out[(2 * side + 1) * count : (2 * side + 2) * count]
        turn_re = turn_ref[0, side, 0]
        turn_im = turn_ref[0, side, 1]
        turned = jnp.concatenate(
            [real * turn_re + imag * turn_im, imag * turn_re - real * turn_im], axis=1
        )
        high, low = split(turned)
        pieces.append(jnp.concatenate([high, high, low], axis=1))
    result = lax.dot_general(
        second_ref[...],
        jnp.concatenate(pieces, axis=0),
        (((1,), (1,)), ((), ())),
        preferred_element_type=F32,
    )
    height = result.shape[0] // len(o_refs)
    for index, o_ref in enumerate(o_refs):
        for side in range(2):
            block = result[
                index * height : (index + 1) * height, side * count : (side + 1) * count
            ]
            o_ref[:, side, 0] = block.reshape(height // SUBLANES, SUBLANES, count)


def row_tables(devices, chunks, sublanes, samples):
    width = chunks * LANES
    inner = sublanes // 2
    count = devices * inner
    lines = width // 2
    freq = iota(count)[:, None]
    order = (inner * iota(devices)[:, None] + iota(inner)[None, :]).reshape(1, devices, inner)
    fc, fs = phases(freq[:, :, None] * order, count)
    bc, bs = phases((freq[:, :, None] + 1) * order, count)
    hc, hs = phases((2 * freq[:, :, None] + 1) * order, 2 * count)
    zero = jnp.zeros_like(fc)
    pack = lambda on_re, on_im: jnp.stack([on_re, on_im], axis=2).reshape(count, devices * sublanes)
    usual = jnp.concatenate([pack(fc, fs), pack(-fs, fc), pack(bc, -bs), pack(-bs, -bc)], axis=0)
    special = jnp.concatenate(
        [pack(fc, zero), pack(-fs, zero), pack(zero, hc), pack(zero, -hs)], axis=0
    )
    high, low = split_xla(jnp.stack([usual, special]))
    first = jnp.concatenate([high, low, high], axis=2)
    beta = (2 * iota(lines)[None, :] + iota(2)[:, None]).reshape(1, width)
    length = count * width
    turn_a = jnp.stack(phases(freq * beta, length))
    turn_b = jnp.stack(phases((freq + 1) * beta, length))
    turn_c = jnp.stack(phases((2 * freq + 1) * beta, 2 * length))
    turn = jnp.stack([jnp.stack([turn_a, turn_b]), jnp.stack([turn_a, turn_c])])
    inside = SUBLANES // 2
    line = (
        SUBLANES * iota(devices)[None, :, None]
        + inside * iota(PARTS)[:, None, None]
        + iota(inside)[None, None, :]
    )
    gc, gs = [
        a.reshape(PARTS, devices, inside, width)
        for a in phases(line.reshape(lines, 1) * beta, width)
    ]
    second = jnp.stack(
        [jnp.concatenate([gc, gs], axis=3), jnp.concatenate([-gs, gc], axis=3)], axis=2
    ).reshape(2 * lines, 2 * width) * (1.0 / math.sqrt(samples))
    high, low = split_xla(second)
    second = jnp.concatenate([high, low, high], axis=1)
    return first, turn, second


def row_stage(arrived, tables, position, part):
    devices, slots, chunks, sublanes, _ = arrived.shape
    first, turn, second = tables
    count = turn.shape[4 - 1]
    variant = jnp.where((iota(slots) == 0) & (position == 0), 1, 0).astype(jnp.int32)
    if part > 0:
        variant = jnp.zeros((slots,), jnp.int32)
    blocks = second.shape[0] // PARTS // SUBLANES
    shape = (blocks, 2, slots, SUBLANES, count)
    return pl.pallas_call(
        row_kernel,
        grid_spec=pltpu.PrefetchScalarGridSpec(
            num_scalar_prefetch=1,
            grid=(slots,),
            in_specs=[
                pl.BlockSpec((devices, 1, chunks, sublanes, LANES), lambda i, v: (0, i, 0, 0, 0)),
                pl.BlockSpec((1,) + first.shape[1:], lambda i, v: (v[i], 0, 0)),
                pl.BlockSpec((1,) + turn.shape[1:], lambda i, v: (v[i], 0, 0, 0, 0)),
                pl.BlockSpec(second.shape, lambda i, v: (0, 0)),
            ],
            out_specs=[
                pl.BlockSpec((blocks, 2, 1, SUBLANES, count), lambda i, v: (0, 0, i, 0, 0))
                for _ in range(PARTS)
            ],
        ),
        out_shape=[jax.ShapeDtypeStruct(shape, F32) for _ in range(PARTS)],
        compiler_params=pltpu.CompilerParams(vmem_limit_bytes=VMEM_LIMIT),
        cost_estimate=pl.CostEstimate(
            flops=slots * 2 * (first.shape[1] * first.shape[2] * chunks * LANES + 2 * count * second.size),
            transcendentals=0,
            bytes_accessed=8 * arrived.size,
        ),
        name="rows",
    )(variant, arrived, first, turn, second)


def band_kernel(taps_ref, o_ref):
    half = LANES // 2
    banded = []
    for drift in range(2):
        for part in range(2):
            line = jnp.broadcast_to(taps_ref[0, 2 * drift + part : 2 * drift + part + 1, :], (half, LANES))
            banded.append(pltpu.roll(line, 0, 1, stride=1, stride_axis=0))
    re = jnp.concatenate([banded[0], banded[2]], axis=0)
    im = jnp.concatenate([banded[1], banded[3]], axis=0)
    lines = jnp.concatenate(
        [jnp.concatenate([re, -im], axis=1), jnp.concatenate([im, re], axis=1)], axis=0
    )
    high, low = split(jnp.transpose(lines))
    o_ref[0] = jnp.concatenate([high, low, high], axis=0)


def band_stage(kernel_re, kernel_im):
    drifts, taps = kernel_re.shape
    lines = jnp.stack([kernel_re, kernel_im], axis=1)
    lines = jnp.pad(lines, ((0, 0), (0, 0), (0, LANES - taps))).reshape(drifts // 2, 4, LANES)
    return pl.pallas_call(
        band_kernel,
        grid=(drifts // 2,),
        in_specs=[pl.BlockSpec((1, 4, LANES), lambda i: (i, 0, 0))],
        out_specs=pl.BlockSpec((1, 6 * LANES, 2 * LANES), lambda i: (i, 0, 0)),
        out_shape=jax.ShapeDtypeStruct((drifts // 2, 6 * LANES, 2 * LANES), BF16),
        name="bands",
    )(lines)


def correlate_kernel(
    devices, counts, pad, inputs, *refs
):
    x_refs, (halo_ref, band_ref) = refs[:inputs], refs[inputs : inputs + 2]
    o_ref, table, last, lhs, stage_a, stage_b = refs[-6:]
    step = pl.program_id(0)
    steps = pl.num_programs(0)
    inside = SUBLANES // 2
    total = 2 * devices * sum(counts)
    pitch = total + pad
    half = LANES // 2
    taps_half = half // 2

    @pl.when(step == 0)
    def _():
        def source(s, carry):
            for part in range(PARTS):
                for side in range(2):
                    for slot in range(counts[part]):
                        x_ref = x_refs[min(part, inputs - 1)]
                        tiles = x_ref.shape[0] // devices // SUBLANES
                        place = side * counts[part] + slot
                        place += 2 * sum(counts[:part]) if inputs < PARTS else 0
                        start = (s * tiles + place) * SUBLANES
                        tile = x_ref[pl.ds(pl.multiple_of(start, SUBLANES), SUBLANES), :]
                        row = devices * sum(counts[:part]) + s * counts[part] + slot
                        if side == 1:
                            row = total - row
                            if slot == 0 and part == 0:
                                row = jnp.where(s == 0, total // 2, row)
                        table[pl.ds(row, SUBLANES, stride=pitch), :] = tile
            return carry

        lax.fori_loop(0, devices, source, 0)
        last[...] = halo_ref[0:2, :]

    lane = lax.broadcasted_iota(jnp.int32, (LANES, LANES), 1)
    row_id = lax.broadcasted_iota(jnp.int32, (LANES, LANES), 0)
    blocks = total // LANES

    def turned(part, line, block):
        start = pl.multiple_of((part * inside + line) * pitch + block * LANES, SUBLANES)
        flat = jnp.transpose(table[pl.ds(start, LANES), :])
        return pltpu.roll(flat, taps_half, 1)

    next_line = jnp.minimum(step + 1, steps - 1)
    for part in range(2):
        rolled = [turned(part, step, block) for block in range(blocks)]
        follow = turned(part, next_line, 0)[0:1, :]
        follow = jnp.where(step == steps - 1, halo_ref[2 + part : 3 + part, :], follow)
        before = jnp.where(row_id == 0, last[part : part + 1, :], pltpu.roll(rolled[-1], 1, 0))
        after = jnp.where(row_id == LANES - 1, follow, pltpu.roll(rolled[0], LANES - 1, 0))
        last[part : part + 1, :] = rolled[-1][LANES - 1 : LANES, :]
        ext = []
        for block in range(blocks + 1):
            left = before if block == 0 else rolled[block - 1]
            right = after if block == blocks else rolled[block]
            ext.append(jnp.where(lane < taps_half, left, right))
        for block in range(blocks):
            odd = jnp.where(
                lane < half, pltpu.roll(ext[block], half, 1), pltpu.roll(ext[block + 1], half, 1)
            )
            for parity, window in enumerate((ext[block], odd)):
                high, low = split(window)
                rows = pl.ds((2 * block + parity) * LANES, LANES)
                lhs[rows, part * LANES : (part + 1) * LANES] = high
                lhs[rows, (2 + part) * LANES : (3 + part) * LANES] = high
                lhs[rows, (4 + part) * LANES : (5 + part) * LANES] = low

    group = 2
    chunks = blocks // group
    drifts = SUBLANES
    span = LANES + SUBLANES

    def multiply(chunk, outer, target):
        rows = pl.ds(pl.multiple_of(chunk * group * 2 * LANES, LANES), group * 2 * LANES)
        windows = lhs[rows, :]
        for pair in range(drifts // 2):
            out = jnp.dot(
                windows, band_ref[outer * drifts // 2 + pair], preferred_element_type=F32
            )
            power = out[:, :LANES] * out[:, :LANES] + out[:, LANES:] * out[:, LANES:]
            for member in range(group):
                even = power[member * 2 * LANES : (member * 2 + 1) * LANES]
                odd = power[(member * 2 + 1) * LANES : (member * 2 + 2) * LANES]
                start = (member * drifts + 2 * pair) * span
                target[start : start + LANES, :] = jnp.where(lane < half, even, pltpu.roll(odd, half, 1))
                start += span
                target[start : start + LANES, :] = jnp.where(lane < half, pltpu.roll(even, half, 1), odd)

    def emit(chunk, outer, origin):
        for member in range(group):
            for line in range(LANES):
                value = origin[pl.ds(member * drifts * span + line, drifts, stride=span), :]
                start = (line * blocks + member + chunk * group) * SUBLANES
                o_ref[outer, pl.ds(pl.multiple_of(start, SUBLANES), SUBLANES), :] = value

    groups = o_ref.shape[0]
    stages = (stage_a, stage_b)

    def body(chunk, carry):
        for outer in range(groups):
            multiply(chunk, outer, stages[outer % 2])
            if outer == 0:
                emit(jnp.maximum(chunk - 1, 0), groups - 1, stages[(groups - 1) % 2])
            else:
                emit(chunk, outer - 1, stages[(outer - 1) % 2])
        return carry

    lax.fori_loop(0, chunks, body, 0)
    emit(chunks - 1, groups - 1, stages[(groups - 1) % 2])


def correlate_stage(arrived, halo, bands, part, earlier, counts):
    devices, _, _, count = arrived[0].shape
    total = 2 * devices * sum(counts)
    drifts = 2 * bands.shape[0]
    groups = drifts // SUBLANES
    pad = SUBLANES
    inside = SUBLANES // 2
    flat = [a.reshape(-1, count) for a in arrived]
    height = count * total // LANES * SUBLANES
    resident = lambda shape: pl.BlockSpec(
        shape, lambda i: (0,) * len(shape), pipeline_mode=pl.Buffered(1)
    )
    extra = [] if earlier is None else [earlier]
    return pl.pallas_call(
        functools.partial(correlate_kernel, devices, counts, pad, len(flat)),
        grid=(inside,),
        in_specs=[resident(a.shape) for a in flat]
        + [resident(halo.shape), resident(bands.shape)]
        + [pl.BlockSpec(memory_space=pl.ANY) for _ in extra],
        out_specs=pl.BlockSpec((groups, height, LANES), lambda i: (0, part * inside + i, 0)),
        out_shape=jax.ShapeDtypeStruct((groups, PARTS * inside * height, LANES), F32),
        input_output_aliases={} if earlier is None else {len(flat) + 2: 0},
        scratch_shapes=[
            pltpu.VMEM(((SUBLANES + 1) * (total + pad), LANES), F32),
            pltpu.VMEM((2, LANES), F32),
            pltpu.VMEM((2 * total // LANES * LANES, 6 * LANES), BF16),
            pltpu.VMEM(((2 * SUBLANES + 1) * (LANES + SUBLANES), LANES), F32),
            pltpu.VMEM(((2 * SUBLANES + 1) * (LANES + SUBLANES), LANES), F32),
        ],
        compiler_params=pltpu.CompilerParams(vmem_limit_bytes=VMEM_LIMIT),
        cost_estimate=pl.CostEstimate(
            flops=inside * 12 * bands.shape[0] * total * count * LANES * 2 // 8,
            transcendentals=0,
            bytes_accessed=groups * inside * height * LANES * 4,
        ),
        name="correlate",
    )(*flat, halo, bands, *extra)


def edge_lines(spectra):
    low, high = spectra
    devices, _, slots, sublanes, count = low.shape
    inside = sublanes // 2
    first = lambda a: a[:, 0, :, ::inside, 0]
    final = lambda a: a[:, 1, :, inside - 1 :: inside, count - 1]
    blank = jnp.zeros_like(first(low)[:1])
    edges = jnp.stack(
        [
            jnp.concatenate([blank, final(high)[:-1]]),
            first(high),
            final(low),
            jnp.concatenate([first(low)[1:], blank]),
        ],
        axis=1,
    )
    edges = jnp.moveaxis(edges, 3, 2).reshape(devices, 1, 8, slots)
    return jnp.pad(edges, ((0, 0), (0, 0), (0, 0), (0, count - slots)))


def halo_lines(edges, slots, taps):
    half = taps // 2
    devices = edges.shape[0]
    lines = jnp.moveaxis(edges[:, :, :slots].reshape(devices, 4, 2, slots), 0, 2)
    lines = lines.reshape(4, 2, devices * slots)
    tail = lambda a: jnp.pad(a[:, half:0:-1], ((0, 0), (0, LANES - half)))
    head = lambda a: jnp.pad(a[:, :half], ((0, 0), (half, LANES - 2 * half)))
    return [
        jnp.concatenate([tail(lines[2 * part]), head(lines[2 * part + 1])], axis=0)
        for part in range(PARTS)
    ]


def tap_kernels(templates, drift_template, drift_reach):
    taps = templates.shape[1] // 2
    selector = (drift_template[:, None] == iota(templates.shape[0])[None, :]).astype(F32)
    chosen = jnp.dot(
        selector, templates, precision=lax.Precision.HIGHEST, preferred_element_type=F32
    )
    index = iota(taps)[None, :]
    center = taps // 2
    inside = (
        (index >= center - drift_reach[:, None]) & (index < center + drift_reach[:, None])
    ).astype(F32)
    return chosen[:, :taps] * inside, chosen[:, taps:] * inside


def fits(shape, devices, drifts, taps):
    rows, cols = shape[1], shape[2]
    lines = devices * cols // LANES
    return (
        2 * LANES // devices == SUBLANES
        and lines // devices == SUBLANES
        and rows % (2 * devices * sum(SHARES)) == 0
        and drifts % SUBLANES == 0
        and 2 * taps == LANES
    )


def local(series, templates, drift_template, drift_reach):
    position = lax.axis_index(AXES)
    devices = lax.axis_size(AXES)
    rows, cols = series.shape[1], series.shape[2]
    taps = templates.shape[1] // 2
    if not fits(series.shape, devices, drift_template.shape[0], taps):
        return general_local(series, templates, drift_template, drift_reach)
    width = devices * cols // LANES
    counts = tuple(rows // 2 // devices * share // sum(SHARES) for share in SHARES)
    samples = 2 * rows * cols * devices
    chunks = 2 * width // LANES
    arrived = []
    swap = lambda value: lax.all_to_all(value, AXES, 0, 0, tiled=True)
    tables = row_tables(devices, chunks, SUBLANES, samples)
    bands = band_stage(*tap_kernels(templates, drift_template, drift_reach))
    for part in range(PARTS):
        columns = column_stage(
            series, position, width, devices * sum(counts[:part]), devices * counts[part]
        )
        columns = columns.reshape(devices, counts[part], chunks, SUBLANES, LANES)
        if part == PARTS - 1:
            columns, bands = lax.optimization_barrier((columns, bands))
        arrived.append(swap(columns))
    pieces = []
    for part in range(PARTS):
        spectra = row_stage(arrived[part], tables, position, part)
        tiles = [a.reshape(devices, 2 * counts[part], SUBLANES, LANES) for a in spectra]
        if part == 0:
            tiles[0] = jnp.concatenate([tiles[0], edge_lines(spectra)], axis=1)
        pieces.append(tiles)
    first = swap(pieces[0][0])
    second = swap(pieces[1][0])
    rest = swap(jnp.concatenate([pieces[0][1], pieces[1][1]], axis=1))
    halos = halo_lines(first[:, 2 * counts[0]], counts[0], taps)
    out = correlate_stage([first, second], halos[0], bands, 0, None, counts)
    out = correlate_stage([rest], halos[1], bands, 1, out, counts)
    groups = out.shape[0]
    out = out.reshape(groups, -1, SUBLANES, LANES)
    return jnp.swapaxes(out, 1, 2).reshape(groups * SUBLANES, -1)


def solution(mesh):
    return jax.shard_map(
        local,
        mesh=mesh,
        in_specs=(P(None, None, AXES), P(), P(), P()),
        out_specs=P(None, AXES),
        check_vma=False,
    )
```
